32 devices in a mesh: site: 2 (over y), owner: 16 (over z, x, core).
Axes of the slice: x: 2, y: 2, z: 4, core: 2. Of those that a mesh axis runs over, the one named last changes fastest.
Arguments:
- green_tensor: bfloat16 [4096, 6, 1024], P(('site', 'owner')), parts along dimension 0, may hold values from -6 to 6
- mechanism: float32 [2, 6, 2048], P(None, None, 'owner'), may hold values from -2.5 to 2.5
- point_owner: int32 [16, 128, 1], P('owner'), may hold values from 0 to 15; in each aligned block of 128 rows (0 to 127, 128 to 255, ..., all dimensions but the last counted through in order) at most 16 rows name the same one
- point_row: int32 [16, 128], P('owner'), may hold values from 0 to 127
- onset_step: int32 [16, 128], P('owner'), may hold values from 0 to 511
- slip_amount: float32 [16, 128], P('owner'), may hold values from 0.01 to 0.1
- point_count: int32 [16], P('owner'), may hold values from 12 to 128
- rake_angle: float32 [16], P('owner'), may hold values from -3.140625 to 3.140625
- slip_rate: float32 [16, 64], P('owner'), may hold values from 0.02 to 0.2
Outputs:
- seismogram: float32 [32, 1024], P(('site', 'owner')), parts along dimension 0
The draws below stay inside these ranges and needn't reach their ends.
There are 2 independent parts, one for each index of `site`. The reference program is written for one: setup_inputs(seed, part) draws one part's arguments, and reference() takes and returns one part's arrays. A program takes and returns all parts, laid end to end along the dimension named above; an argument that names none is the same for every part. Nothing has to cross between parts.
Inputs may be any that keep to these rules, and one draw needn't show every extreme that they name: `point_owner`: among the 128 entries of one device's variations, at most 16 name the same owner, a bound that some block reaches of them.
All inputs are finite; a program needn't handle non-finite values.
Results may differ from the reference program's by a relative error of at most 0.0029.
Values may be sent and summed in bfloat16 or wider, within the bound.
No kernel may reach another device: no remote copies, remote signals or barrier semaphores. Data moves between devices by JAX's collectives and lax.ppermute only.
A program may use at most 64 MiB of HBM per device.

```python
import math
import jax
import jax.numpy as jnp
import numpy as np
from jax import lax

T_SIZE = 1024
K = 64
P_DEV = 128
V_DEV = 1
LMAX = 128
POINTS = 2048
VARS = 16
OMAX = 512
CAP = 16
N_OWNER = 16


def set_ends(values, rng, least, high):
    longest = values.shape.index(max(values.shape))
    spots = []
    for shift in (0, 1):
        where = [jax.random.randint(jax.random.fold_in(rng, axis), (), 0, length) for axis, length in enumerate(values.shape)]
        where[longest] = (where[longest] + shift) % values.shape[longest]
        spots.append(tuple(where))
    return values.at[spots[0]].set(least).at[spots[1]].set(high)


def block_levels(key, extent, split, least, high):
    def one(dim, blocks):
        heights = jax.random.uniform(jax.random.fold_in(jax.random.fold_in(key, 6), dim), (blocks,), jnp.float32, least / len(split), high / len(split))
        return jnp.repeat(jnp.exp(heights), extent[dim] // blocks).reshape((-1,) + (1,) * (len(extent) - dim - 1))

    factor_of = one(*split[0])
    for cut in split[1:]:
        factor_of = factor_of * one(*cut)
    return factor_of


def routed_block(own_key, own, number, rows, number_of, top, limit, skew):
    sequence = jax.random.permutation(own_key, number_of)
    heavy_load, usual = load_shares(number_of, rows * top, limit, skew, True), load_shares(number_of, rows * top, limit, skew, False)
    places = jnp.arange(number_of)

    def named(tallies, rotation):
        used = int((tallies > 0).sum())
        fixed = max(1, used // 4)
        passed = fixed + (places - fixed + rotation * (used - fixed)) % max(1, number_of - fixed)
        return jnp.zeros((number_of,), jnp.int32).at[sequence[jnp.where(places < fixed, places, passed)]].set(jnp.asarray(tallies, jnp.int32))

    tallies = jnp.where(number % 4 == 0, named(heavy_load, number // 4), named(usual, number - number // 4 - 1))
    mixed = jax.random.permutation(jax.random.fold_in(own, 3), number_of)
    donor, sink = mixed[0:number_of // 2 * 2:2], mixed[1:number_of // 2 * 2:2]
    slack = jnp.minimum(tallies[donor] - 1, limit - tallies[sink]) // 2
    slack = jnp.where((donor == sequence[0]) | (sink == sequence[0]) | (tallies[sink] == 0), 0, jnp.maximum(slack, 0))
    passed = jax.random.randint(jax.random.fold_in(own, 4), (number_of // 2,), 0, 1 << 20) % (slack + 1)
    tallies = tallies.at[donor].add(-passed).at[sink].add(passed)
    members = jnp.searchsorted(jnp.cumsum(tallies), jnp.arange(rows * top), side="right").astype(jnp.int32)
    table = members.reshape(top, rows).T
    table = table[jax.random.permutation(jax.random.fold_in(own, 1), rows)]
    rotation = jax.random.randint(jax.random.fold_in(own, 2), (rows, 1), 0, top)
    return jnp.take_along_axis(table, (jnp.arange(top)[None, :] + rotation) % top, axis=1)


def load_shares(count, total, reach, skew, full):
    weights = [(1 << 20) // math.isqrt(standing ** skew) + 1 for standing in range(1, count + 1)]
    largest = reach if full else min(reach, max(-(-total // count), total * weights[0] // sum(weights)))
    least = 1 if total - largest >= count - 1 else 0
    given, rest = [largest] + [least] * (count - 1), total - largest - least * (count - 1)
    while rest > 0:
        candidates = [i for i in range(1, count) if given[i] < largest] or [i for i in range(1, count) if given[i] < reach]
        pool, budget = sum([weights[i] for i in candidates]), rest
        for i in candidates:
            addition = min(reach - given[i], max(1, budget * weights[i] // pool), rest)
            given[i] = given[i] + addition
            rest = rest - addition
    return np.array(given)


def noise(rng, dims, scale, limit, cuts=(), held_as=jnp.bfloat16):
    entries = jax.random.normal(rng, dims, jnp.float32) * scale
    if len(cuts) > 0:
        entries = block_levels(rng, dims, cuts, -0.22, 0.18) * entries
    return jnp.clip(entries, min=-limit, max=limit).astype(held_as)


def setup_inputs(seed: int = 0, part: int = 0) -> dict:
    splits = jax.random.split(jax.random.key(seed), 10)
    part_keys = jax.random.split(jax.random.fold_in(splits[9], part), 10)
    green_tensor = noise(part_keys[0], (POINTS, 6, T_SIZE), 1.0, 6.0, ((0, 16),))
    mechanism = noise(splits[1], (2, 6, POINTS), 6 ** -0.5, 2.5, ((2, 16),), jnp.float32)
    point_owner_keys = jax.random.split(jax.random.fold_in(splits[2], 1), VARS * LMAX // (V_DEV * LMAX))
    point_owner_turns = jax.random.permutation(jax.random.fold_in(splits[2], 3), VARS * LMAX // (V_DEV * LMAX))
    point_owner = jax.vmap(lambda own, number: routed_block(jax.random.fold_in(splits[2], 2), own, number, V_DEV * LMAX, N_OWNER, 1, CAP, 2))(point_owner_keys, point_owner_turns).reshape((VARS, LMAX, 1))
    point_row = set_ends(jax.random.randint(splits[3], (VARS, LMAX), 0, P_DEV), jax.random.fold_in(splits[3], 1), 0, P_DEV - 1).astype(jnp.int32)
    onset_step = set_ends(jax.random.randint(splits[4], (VARS, LMAX), 0, OMAX), jax.random.fold_in(splits[4], 1), 0, OMAX - 1).astype(jnp.int32)
    slip_amount = jnp.clip(jnp.exp(math.log(0.1) - 2.3025851 * jax.random.uniform(splits[5], (VARS, LMAX), jnp.float32) ** block_levels(splits[5], (VARS, LMAX), ((0, 16),), -0.2, 0.2)), 0.01, 0.1)
    point_count = set_ends(jax.random.randint(splits[6], (VARS,), LMAX // 10, LMAX + 1), jax.random.fold_in(splits[6], 1), LMAX // 10, LMAX).astype(jnp.int32)
    rake_angle = jnp.clip(jax.random.uniform(splits[7], (VARS,), jnp.float32, -3.140625, 3.140625), -3.140625, 3.140625)
    slip_rate = jnp.clip(jnp.exp(math.log(0.2) - 2.3025851 * jax.random.uniform(splits[8], (VARS, K), jnp.float32) ** block_levels(splits[8], (VARS, K), ((0, 16),), -0.2, 0.2)), 0.02, 0.2)
    return {"green_tensor": green_tensor, "mechanism": mechanism, "point_owner": point_owner, "point_row": point_row, "onset_step": onset_step, "slip_amount": slip_amount, "point_count": point_count, "rake_angle": rake_angle, "slip_rate": slip_rate}


def delay_traces(traces, steps):
    length = traces.shape[-1]
    source_step = jnp.arange(length, dtype=jnp.int32) - steps[..., None]
    inside = source_step >= 0
    time_index = jnp.broadcast_to(jnp.maximum(source_step, 0)[..., None, :], traces.shape)
    moved = jnp.take_along_axis(traces, time_index, axis=-1)
    return jnp.where(inside[..., None, :], moved, jnp.zeros_like(moved))


def smooth(signal, kernel):
    taps = kernel.shape[1]
    filtered = lax.conv_general_dilated(signal[None], kernel[:, None, ::-1], (1,), ((taps - 1, 0),), dimension_numbers=("NCH", "OIH", "NCH"), feature_group_count=signal.shape[0], precision=lax.Precision.HIGHEST)
    return filtered[0]


def project(green_block, mech_block):
    return jnp.einsum("kcp,pct->pkt", mech_block, green_block.astype(jnp.float32), precision=lax.Precision.HIGHEST).astype(jnp.bfloat16)


def coefficients(slip_amount, point_count, rake_angle):
    length = slip_amount.shape[1]
    alive_mask = jnp.arange(length, dtype=jnp.int32)[None, :] < point_count[:, None]
    weight = jnp.where(alive_mask, slip_amount, jnp.zeros_like(slip_amount))
    return jnp.stack([jnp.cos(rake_angle)[:, None] * weight, jnp.sin(rake_angle)[:, None] * weight], axis=2)


def reference(green_tensor, mechanism, point_owner, point_row, onset_step, slip_amount, point_count, rake_angle, slip_rate):
    def project_pair(pair):
        return project(pair[0], pair[1])

    blocks = lax.map(project_pair, (green_tensor.reshape(N_OWNER, P_DEV, 6, T_SIZE), jnp.transpose(mechanism.reshape(2, 6, N_OWNER, P_DEV), (2, 0, 1, 3))))
    traces = blocks.reshape(N_OWNER * P_DEV, 2, T_SIZE)
    coefficient = coefficients(slip_amount, point_count, rake_angle)
    point_index = (point_owner[:, :, 0] * P_DEV + point_row).astype(jnp.int32)

    def one_variation(items):
        index_row, delay_row, coef_row = items
        shifted = delay_traces(traces[index_row], delay_row)
        return jnp.sum(shifted.astype(jnp.float32) * coef_row[:, :, None], axis=(0, 1))

    summed = lax.map(one_variation, (point_index, onset_step, coefficient))
    return smooth(summed, slip_rate)
```

```python
import functools

import jax
import jax.numpy as jnp
from jax import lax
from jax.experimental import pallas as pl
from jax.experimental.pallas import tpu as pltpu
from jax.sharding import PartitionSpec as P

LANES = 128
FIELDS = 4
VMEM = pl.BlockSpec(memory_space=pltpu.VMEM)
SMEM = pl.BlockSpec(memory_space=pltpu.SMEM)


def route_kernel(capacity, rows, count_ref, rake_ref, owner_ref, row_ref, onset_ref, slip_ref, out_ref):
    owners = out_ref.shape[0]
    length = row_ref.shape[1]
    lane = lax.broadcasted_iota(jnp.int32, (1, length), 1)
    alive = lane < count_ref[0]
    onset = onset_ref[...]
    whole = onset // LANES
    base = row_ref[...] * (4 * rows) + rows - whole
    rake = jnp.full((1, length), rake_ref[0], jnp.float32)
    weight = jnp.where(alive, slip_ref[...], 0.0)
    fields = (
        base.astype(jnp.float32),
        (onset - whole * LANES).astype(jnp.float32),
        jnp.cos(rake) * weight,
        jnp.sin(rake) * weight,
    )
    owner_index = lax.broadcasted_iota(jnp.int32, (owners, length), 0)
    hot = ((owner_index == owner_ref[...]) & alive).astype(jnp.float32)
    earlier = lax.broadcasted_iota(jnp.int32, (length, length), 0) < lax.broadcasted_iota(
        jnp.int32, (length, length), 1
    )
    before = jnp.dot(hot, earlier.astype(jnp.float32), preferred_element_type=jnp.float32)
    rank = jnp.sum(hot * before, axis=0, keepdims=True).astype(jnp.int32)
    place = lax.broadcasted_iota(jnp.int32, (LANES, length), 0)
    spread = jnp.zeros((LANES, length), jnp.float32)
    for number, field in enumerate(fields):
        spread = jnp.where(place == rank + number * capacity, field, spread)
    out_ref[...] = lax.dot_general(
        hot,
        spread,
        (((1,), (1,)), ((), ())),
        precision=lax.Precision.HIGHEST,
        preferred_element_type=jnp.float32,
    )


def project_kernel(rows, mech_ref, green_ref, out_ref, flat_ref, column_ref):
    parts, points, _ = green_ref.shape
    flat_ref[...] = jnp.zeros_like(flat_ref)
    for part in range(parts):
        for kind in range(2):
            flat_ref[2 * part + kind : 2 * part + kind + 1, :] = mech_ref[part, kind : kind + 1, :]
    column_ref[...] = flat_ref[...].T
    group = 16
    blank = jnp.zeros((rows, LANES), jnp.float32)

    def clear(number, carry):
        out_ref[pl.ds(pl.multiple_of(number * 2 * rows, rows), rows), :] = blank
        return carry

    lax.fori_loop(0, 2 * points, clear, 0, unroll=8)

    def one(number, carry):
        first = pl.multiple_of(number * group, group)
        scale = [
            jnp.broadcast_to(column_ref[pl.ds(first, group), i : i + 1], (group, LANES))
            for i in range(2 * parts)
        ]
        for step in range(rows):
            total = [jnp.zeros((group, LANES), jnp.float32)] * 2
            for part in range(parts):
                block = green_ref[part, pl.ds(first, group), step * LANES : (step + 1) * LANES].astype(
                    jnp.float32
                )
                total = [total[kind] + scale[2 * part + kind] * block for kind in range(2)]
            for kind in range(2):
                kept = total[kind].astype(jnp.bfloat16).astype(jnp.float32)
                for half in range(group // 8):
                    start = (first + half * 8) * (4 * rows) + kind * 2 * rows + rows + step
                    out_ref[pl.ds(start, 8, stride=4 * rows), :] = kept[half * 8 : half * 8 + 8]
        return carry

    lax.fori_loop(0, points // group, one, 0)


def gather_kernel(capacity, rows, table_ref, trace_ref, out_ref):
    lane = lax.broadcasted_iota(jnp.int32, (rows, LANES), 1)

    def one(number, carry):
        total = jnp.zeros((rows, LANES), jnp.float32)
        for slot in range(capacity):
            place = number * LANES + slot
            base = table_ref[place].astype(jnp.int32)
            shift = table_ref[place + capacity].astype(jnp.int32)
            first = table_ref[place + 2 * capacity]
            second = table_ref[place + 3 * capacity]
            base = jnp.maximum(base, 1)
            stays = lane < LANES - shift
            one_kind = jnp.where(
                stays, trace_ref[pl.ds(base, rows), :], trace_ref[pl.ds(base - 1, rows), :]
            )
            base = base + 2 * rows
            other_kind = jnp.where(
                stays, trace_ref[pl.ds(base, rows), :], trace_ref[pl.ds(base - 1, rows), :]
            )
            total = total + pltpu.roll(one_kind * first + other_kind * second, shift, 1)
        out_ref[number] = total
        return carry

    lax.fori_loop(0, out_ref.shape[0], one, 0)


def smooth_kernel(taps, rate_ref, part_ref, out_ref):
    signal = jnp.sum(part_ref[...], axis=0)
    rows = signal.shape[0]
    row = lax.broadcasted_iota(jnp.int32, (rows, LANES), 0)
    lane = lax.broadcasted_iota(jnp.int32, (rows, LANES), 1)
    previous = jnp.where(row == 0, 0.0, pltpu.roll(signal, 1, 0))
    total = [signal * rate_ref[0]] + [jnp.zeros_like(signal)] * 3
    for tap in range(1, taps):
        moved = pltpu.roll(jnp.where(lane < LANES - tap, signal, previous), tap, 1)
        total[tap % 4] = total[tap % 4] + moved * rate_ref[tap]
    out_ref[...] = (total[0] + total[1]) + (total[2] + total[3])


def local(
    green_tensor,
    mechanism,
    point_owner,
    point_row,
    onset_step,
    slip_amount,
    point_count,
    rake_angle,
    slip_rate,
):
    owners = lax.axis_size("owner")
    variations, length = point_row.shape
    points, parts, steps = green_tensor.shape
    taps = slip_rate.shape[1]
    rows = steps // LANES
    capacity = 2 * length // owners
    assert variations == 1 and capacity * FIELDS <= LANES
    table = pl.pallas_call(
        functools.partial(route_kernel, capacity, rows),
        out_shape=jax.ShapeDtypeStruct((owners, LANES), jnp.float32),
        in_specs=[SMEM, SMEM, VMEM, VMEM, VMEM, VMEM],
        out_specs=VMEM,
        name="route",
    )(point_count, rake_angle, point_owner.reshape(1, length), point_row, onset_step, slip_amount)
    table = lax.all_to_all(
        table.reshape(owners, 1, LANES), "owner", split_axis=0, concat_axis=0, tiled=True
    )
    traces = pl.pallas_call(
        functools.partial(project_kernel, rows),
        out_shape=jax.ShapeDtypeStruct((points * 4 * rows, LANES), jnp.float32),
        in_specs=[VMEM, VMEM],
        out_specs=VMEM,
        scratch_shapes=[pltpu.VMEM((LANES, points), jnp.float32), pltpu.VMEM((points, LANES), jnp.float32)],
        name="project",
    )(jnp.transpose(mechanism, (1, 0, 2)), jnp.transpose(green_tensor, (1, 0, 2)))
    partial = pl.pallas_call(
        functools.partial(gather_kernel, capacity, rows),
        out_shape=jax.ShapeDtypeStruct((owners, rows, LANES), jnp.float32),
        in_specs=[SMEM, VMEM],
        out_specs=VMEM,
        name="gather",
    )(table.reshape(owners * LANES), traces)
    partial = lax.all_to_all(partial, "owner", split_axis=0, concat_axis=0, tiled=True)
    result = pl.pallas_call(
        functools.partial(smooth_kernel, taps),
        out_shape=jax.ShapeDtypeStruct((rows, LANES), jnp.float32),
        in_specs=[SMEM, VMEM],
        out_specs=VMEM,
        name="smooth",
    )(slip_rate.reshape(taps), partial)
    return result.reshape(1, steps)


def solution(mesh):
    in_specs = (
        P(("site", "owner"), None, None),
        P(None, None, "owner"),
        P("owner", None, None),
        P("owner", None),
        P("owner", None),
        P("owner", None),
        P("owner"),
        P("owner"),
        P("owner", None),
    )
    out_specs = P(("site", "owner"), None)
    return jax.shard_map(local, mesh=mesh, in_specs=in_specs, out_specs=out_specs, check_vma=False)
```

```python
import functools

import jax
import jax.numpy as jnp
from jax import lax
from jax.experimental import pallas as pl
from jax.experimental.pallas import tpu as pltpu
from jax.sharding import PartitionSpec as P

LANES = 128
FIELDS = 4
ANY = pl.BlockSpec(memory_space=pltpu.HBM)
VMEM = pl.BlockSpec(memory_space=pltpu.VMEM)
SMALL = pltpu.CompilerParams(vmem_limit_bytes=16 << 20)


def in_hbm(array):
    return pltpu.with_memory_space_constraint(array, pltpu.HBM)


def in_vmem(array):
    return pltpu.with_memory_space_constraint(array, pltpu.VMEM)


def fetch(sources, targets, arrived):
    copies = [
        pltpu.make_async_copy(source, target, arrived.at[number])
        for number, (source, target) in enumerate(zip(sources, targets))
    ]
    for copy in copies:
        copy.start()
    for copy in copies:
        copy.wait()


def route_kernel(capacity, rows, *refs):
    sources, out_ref, targets, arrived = refs[:6], refs[6], refs[7:13], refs[13]
    fetch(sources, targets, arrived)
    owner_ref, row_ref, onset_ref, slip_ref, count_ref, rake_ref = targets
    owners = out_ref.shape[0]
    length = row_ref.shape[1]
    lane = lax.broadcasted_iota(jnp.int32, (1, length), 1)
    alive = lane < count_ref[0]
    onset = onset_ref[...]
    whole = onset // LANES
    base = row_ref[...] * (4 * rows) + (rows - 1) - whole
    rake = jnp.full((1, length), rake_ref[0], jnp.float32)
    weight = jnp.where(alive, slip_ref[...], 0.0)
    fields = (
        base.astype(jnp.float32),
        (onset - whole * LANES).astype(jnp.float32),
        jnp.cos(rake) * weight,
        jnp.sin(rake) * weight,
    )
    owner_index = lax.broadcasted_iota(jnp.int32, (owners, length), 0)
    hot = ((owner_index == owner_ref[...]) & alive).astype(jnp.float32)
    earlier = lax.broadcasted_iota(jnp.int32, (length, length), 0) < lax.broadcasted_iota(
        jnp.int32, (length, length), 1
    )
    before = jnp.dot(hot, earlier.astype(jnp.float32), preferred_element_type=jnp.float32)
    rank = jnp.sum(hot * before, axis=0, keepdims=True).astype(jnp.int32)
    place = lax.broadcasted_iota(jnp.int32, (LANES, length), 0)
    spread = jnp.zeros((LANES, length), jnp.float32)
    for number, field in enumerate(fields):
        spread = jnp.where(place == rank + number * capacity, field, spread)
    out_ref[...] = lax.dot_general(
        hot,
        spread,
        (((1,), (1,)), ((), ())),
        precision=lax.Precision.HIGHEST,
        preferred_element_type=jnp.float32,
    )


def project_kernel(
    rows, group, chunk, mech_ref, rate_ref, green_ref, out_ref, rates_ref,
    mech_here, rate_here, green_here, flat_ref, column_ref, arrived, landed,
):
    parts, points, _ = green_ref.shape
    small = [
        pltpu.make_async_copy(mech_ref, mech_here, arrived.at[0]),
        pltpu.make_async_copy(rate_ref, rate_here, arrived.at[1]),
    ]
    large = [
        pltpu.make_async_copy(
            green_ref.at[:, pl.ds(first, chunk), :], green_here.at[:, pl.ds(first, chunk), :], landed.at[number]
        )
        for number, first in enumerate(range(0, points, chunk))
    ]
    for copy in small + large:
        copy.start()
    blank = jnp.zeros((rows, LANES), jnp.float32)

    def clear(number, carry):
        out_ref[pl.ds(pl.multiple_of(number * 2 * rows, rows), rows), :] = blank
        return carry

    lax.fori_loop(0, 2 * points, clear, 0, unroll=8)
    flat_ref[...] = jnp.zeros_like(flat_ref)
    for copy in small:
        copy.wait()
    taps = rate_here.shape[1]
    for part in range(parts):
        for kind in range(2):
            flat_ref[2 * part + kind : 2 * part + kind + 1, :] = mech_here[part, kind : kind + 1, :]
    flat_ref[2 * parts : 2 * parts + 1, 0:taps] = rate_here[...]
    column_ref[...] = flat_ref[...].T
    rates_ref[...] = jnp.broadcast_to(column_ref[0:taps, 2 * parts : 2 * parts + 1], (taps, LANES))

    def one(number, carry):
        first = pl.multiple_of(number * group, group)
        scale = [
            jnp.broadcast_to(column_ref[pl.ds(first, group), i : i + 1], (group, LANES))
            for i in range(2 * parts)
        ]
        for step in range(rows):
            total = [jnp.zeros((group, LANES), jnp.float32)] * 2
            for part in range(parts):
                block = green_here[part, pl.ds(first, group), step * LANES : (step + 1) * LANES].astype(
                    jnp.float32
                )
                total = [total[kind] + scale[2 * part + kind] * block for kind in range(2)]
            for kind in range(2):
                kept = total[kind].astype(jnp.bfloat16).astype(jnp.float32)
                for half in range(group // 8):
                    start = (first + half * 8) * (4 * rows) + kind * 2 * rows + rows + step
                    out_ref[pl.ds(start, 8, stride=4 * rows), :] = kept[half * 8 : half * 8 + 8]
        return carry

    for number, copy in enumerate(large):
        copy.wait()
        lax.fori_loop(number * (chunk // group), (number + 1) * (chunk // group), one, 0)


def gather_kernel(capacity, rows, sent_ref, trace_ref, out_ref, word_here, word_ref, scale_ref, arrived):
    scales = pltpu.make_async_copy(sent_ref, scale_ref, arrived.at[0])
    scales.start()
    sent = sent_ref[...]
    whole = (sent + 0.5).astype(jnp.int32)
    word_here[...] = whole * LANES + pltpu.roll(whole, LANES - capacity, 1)
    words = pltpu.make_async_copy(word_here, word_ref, arrived.at[1])
    words.start()
    left = LANES - 1 - lax.broadcasted_iota(jnp.int32, (rows, LANES), 1)
    scales.wait()
    words.wait()
    for number in range(out_ref.shape[0]):
        total = [jnp.zeros((rows, LANES), jnp.float32)] * 2
        for slot in range(capacity):
            word = word_ref[number, slot]
            first = scale_ref[number, slot + 2 * capacity]
            second = scale_ref[number, slot + 3 * capacity]
            base = word // LANES
            shift = word & (LANES - 1)
            stays = left >= shift
            one_kind = jnp.where(
                stays, trace_ref[pl.ds(base + 1, rows), :], trace_ref[pl.ds(base, rows), :]
            )
            base = base + 2 * rows
            other_kind = jnp.where(
                stays, trace_ref[pl.ds(base + 1, rows), :], trace_ref[pl.ds(base, rows), :]
            )
            moved = pltpu.roll(one_kind * first + other_kind * second, shift, 1)
            total[slot % 2] = total[slot % 2] + moved
        out_ref[number] = total[0] + total[1]


def smooth_kernel(rates_ref, part_ref, out_ref):
    signal = jnp.sum(part_ref[...], axis=0)
    taps = rates_ref.shape[0]
    rows = signal.shape[0]
    row = lax.broadcasted_iota(jnp.int32, (rows, LANES), 0)
    lane = lax.broadcasted_iota(jnp.int32, (rows, LANES), 1)
    previous = jnp.where(row == 0, 0.0, pltpu.roll(signal, 1, 0))
    total = [jnp.zeros_like(signal)] * 4
    for tap in range(taps):
        moved = signal
        if tap > 0:
            moved = pltpu.roll(jnp.where(lane < LANES - tap, signal, previous), tap, 1)
        total[tap % 4] = total[tap % 4] + moved * rates_ref[tap : tap + 1, :]
    out_ref[...] = (total[0] + total[1]) + (total[2] + total[3])


def local(
    green_tensor,
    mechanism,
    point_owner,
    point_row,
    onset_step,
    slip_amount,
    point_count,
    rake_angle,
    slip_rate,
):
    owners = lax.axis_size("owner")
    variations, length = point_row.shape
    points, parts, steps = green_tensor.shape
    taps = slip_rate.shape[1]
    rows = steps // LANES
    capacity = 2 * length // owners
    assert variations == 1 and capacity * FIELDS <= LANES
    listed = [point_owner.reshape(1, length), point_row, onset_step, slip_amount, point_count, rake_angle]
    table = pl.pallas_call(
        functools.partial(route_kernel, capacity, rows),
        out_shape=jax.ShapeDtypeStruct((owners, LANES), jnp.float32),
        in_specs=[ANY] * 6,
        out_specs=VMEM,
        scratch_shapes=[pltpu.VMEM((1, length), array.dtype) for array in listed[:4]]
        + [pltpu.SMEM((1,), jnp.int32), pltpu.SMEM((1,), jnp.float32), pltpu.SemaphoreType.DMA((6,))],
        compiler_params=SMALL,
        name="route",
    )(*[in_hbm(array) for array in listed[:4]], *listed[4:])
    table = lax.all_to_all(
        table.reshape(owners, 1, LANES), "owner", split_axis=0, concat_axis=0, tiled=True
    )
    group, chunk = 16, 32
    traces, rates = pl.pallas_call(
        functools.partial(project_kernel, rows, group, chunk),
        out_shape=(
            pltpu.VMEM((points * 4 * rows, LANES), jnp.float32),
            pltpu.VMEM((taps, LANES), jnp.float32),
        ),
        in_specs=[ANY] * 3,
        out_specs=(VMEM, VMEM),
        scratch_shapes=[
            pltpu.VMEM((parts, 2, points), jnp.float32),
            pltpu.VMEM((1, taps), jnp.float32),
            pltpu.VMEM((parts, points, steps), jnp.bfloat16),
            pltpu.VMEM((LANES, points), jnp.float32),
            pltpu.VMEM((points, LANES), jnp.float32),
            pltpu.SemaphoreType.DMA((2,)),
            pltpu.SemaphoreType.DMA((points // chunk,)),
        ],
        compiler_params=SMALL,
        name="project",
    )(
        in_hbm(jnp.transpose(mechanism, (1, 0, 2))),
        in_hbm(slip_rate),
        in_hbm(jnp.transpose(green_tensor, (1, 0, 2))),
    )
    partial = pl.pallas_call(
        functools.partial(gather_kernel, capacity, rows),
        out_shape=pltpu.VMEM((owners, rows, LANES), jnp.float32),
        in_specs=[VMEM, VMEM],
        out_specs=VMEM,
        scratch_shapes=[
            pltpu.VMEM((owners, LANES), jnp.int32),
            pltpu.SMEM((owners, LANES), jnp.int32),
            pltpu.SMEM((owners, LANES), jnp.float32),
            pltpu.SemaphoreType.DMA((2,)),
        ],
        compiler_params=SMALL,
        name="gather",
    )(in_vmem(table.reshape(owners, LANES)), in_vmem(traces))
    partial = lax.all_to_all(partial, "owner", split_axis=0, concat_axis=0, tiled=True)
    result = pl.pallas_call(
        smooth_kernel,
        out_shape=jax.ShapeDtypeStruct((rows, LANES), jnp.float32),
        in_specs=[VMEM, VMEM],
        out_specs=VMEM,
        compiler_params=SMALL,
        name="smooth",
    )(in_vmem(rates), in_vmem(partial))
    return result.reshape(1, steps)


def solution(mesh):
    in_specs = (
        P(("site", "owner"), None, None),
        P(None, None, "owner"),
        P("owner", None, None),
        P("owner", None),
        P("owner", None),
        P("owner", None),
        P("owner"),
        P("owner"),
        P("owner", None),
    )
    out_specs = P(("site", "owner"), None)
    return jax.shard_map(local, mesh=mesh, in_specs=in_specs, out_specs=out_specs, check_vma=False)
```

```python
import functools

import jax
import jax.numpy as jnp
from jax import lax
from jax.experimental import pallas as pl
from jax.experimental.pallas import tpu as pltpu
from jax.sharding import PartitionSpec as P

LANES = 128
FIELDS = 4
ANY = pl.BlockSpec(memory_space=pltpu.HBM)
SMEM = pl.BlockSpec(memory_space=pltpu.SMEM)
VMEM = pl.BlockSpec(memory_space=pltpu.VMEM)
SMALL = pltpu.CompilerParams(vmem_limit_bytes=16 << 20)


def in_hbm(array):
    return pltpu.with_memory_space_constraint(array, pltpu.HBM)


def in_vmem(array):
    return pltpu.with_memory_space_constraint(array, pltpu.VMEM)


def fetch(sources, targets, arrived):
    copies = [
        pltpu.make_async_copy(source, target, arrived.at[number])
        for number, (source, target) in enumerate(zip(sources, targets))
    ]
    for copy in copies:
        copy.start()
    for copy in copies:
        copy.wait()


def route_kernel(capacity, rows, *refs):
    count_ref, rake_ref, sources, out_ref, targets, arrived = (
        refs[0], refs[1], refs[2:6], refs[6], refs[7:11], refs[11]
    )
    fetch(sources, targets, arrived)
    owner_ref, row_ref, onset_ref, slip_ref = targets
    owners = out_ref.shape[0]
    length = row_ref.shape[1]
    lane = lax.broadcasted_iota(jnp.int32, (1, length), 1)
    alive = lane < count_ref[0]
    onset = onset_ref[...]
    whole = onset // LANES
    base = row_ref[...] * (4 * rows) + (rows - 1) - whole
    rake = jnp.full((1, length), rake_ref[0], jnp.float32)
    weight = jnp.where(alive, slip_ref[...], 0.0)
    fields = (
        base.astype(jnp.float32),
        (onset - whole * LANES).astype(jnp.float32),
        jnp.cos(rake) * weight,
        jnp.sin(rake) * weight,
    )
    owner_index = lax.broadcasted_iota(jnp.int32, (owners, length), 0)
    hot = ((owner_index == owner_ref[...]) & alive).astype(jnp.float32)
    earlier = lax.broadcasted_iota(jnp.int32, (length, length), 0) < lax.broadcasted_iota(
        jnp.int32, (length, length), 1
    )
    before = jnp.dot(hot, earlier.astype(jnp.float32), preferred_element_type=jnp.float32)
    rank = jnp.sum(hot * before, axis=0, keepdims=True).astype(jnp.int32)
    place = lax.broadcasted_iota(jnp.int32, (LANES, length), 0)
    spread = jnp.zeros((LANES, length), jnp.float32)
    for number, field in enumerate(fields):
        spread = jnp.where(place == rank + number * capacity, field, spread)
    out_ref[...] = lax.dot_general(
        hot,
        spread,
        (((1,), (1,)), ((), ())),
        precision=lax.Precision.HIGHEST,
        preferred_element_type=jnp.float32,
    )


def project_kernel(
    rows, group, chunk, mech_ref, rate_ref, green_ref, out_ref, rates_ref,
    mech_here, rate_here, green_here, flat_ref, column_ref, arrived, landed,
):
    parts, points, _ = green_ref.shape
    small = [
        pltpu.make_async_copy(mech_ref, mech_here, arrived.at[0]),
        pltpu.make_async_copy(rate_ref, rate_here, arrived.at[1]),
    ]
    large = [
        pltpu.make_async_copy(
            green_ref.at[:, pl.ds(first, chunk), :], green_here.at[:, pl.ds(first, chunk), :], landed.at[number]
        )
        for number, first in enumerate(range(0, points, chunk))
    ]
    for copy in small + large:
        copy.start()
    blank = jnp.zeros((rows, LANES), jnp.float32)

    def clear(number, carry):
        out_ref[pl.ds(pl.multiple_of(number * 2 * rows, rows), rows), :] = blank
        return carry

    lax.fori_loop(0, 2 * points, clear, 0, unroll=8)
    flat_ref[...] = jnp.zeros_like(flat_ref)
    for copy in small:
        copy.wait()
    taps = rate_here.shape[1]
    for part in range(parts):
        for kind in range(2):
            flat_ref[2 * part + kind : 2 * part + kind + 1, :] = mech_here[part, kind : kind + 1, :]
    flat_ref[2 * parts : 2 * parts + 1, 0:taps] = rate_here[...]
    column_ref[...] = flat_ref[...].T
    rates_ref[...] = jnp.broadcast_to(column_ref[0:taps, 2 * parts : 2 * parts + 1], (taps, LANES))

    def one(number, carry):
        first = pl.multiple_of(number * group, group)
        scale = [
            jnp.broadcast_to(column_ref[pl.ds(first, group), i : i + 1], (group, LANES))
            for i in range(2 * parts)
        ]
        for step in range(rows):
            total = [jnp.zeros((group, LANES), jnp.float32)] * 2
            for part in range(parts):
                block = green_here[part, pl.ds(first, group), step * LANES : (step + 1) * LANES].astype(
                    jnp.float32
                )
                total = [total[kind] + scale[2 * part + kind] * block for kind in range(2)]
            for kind in range(2):
                kept = total[kind].astype(jnp.bfloat16).astype(jnp.float32)
                for half in range(group // 8):
                    start = (first + half * 8) * (4 * rows) + kind * 2 * rows + rows + step
                    out_ref[pl.ds(start, 8, stride=4 * rows), :] = kept[half * 8 : half * 8 + 8]
        return carry

    for number, copy in enumerate(large):
        copy.wait()
        lax.fori_loop(number * (chunk // group), (number + 1) * (chunk // group), one, 0)


def gather_kernel(capacity, rows, sent_ref, trace_ref, out_ref, word_here, word_ref, scale_ref, arrived):
    scales = pltpu.make_async_copy(sent_ref, scale_ref, arrived.at[0])
    scales.start()
    sent = sent_ref[...]
    whole = (sent + 0.5).astype(jnp.int32)
    word_here[...] = whole * LANES + pltpu.roll(whole, LANES - capacity, 1)
    words = pltpu.make_async_copy(word_here, word_ref, arrived.at[1])
    words.start()
    left = LANES - 1 - lax.broadcasted_iota(jnp.int32, (rows, LANES), 1)
    scales.wait()
    words.wait()
    for number in range(out_ref.shape[0]):
        total = [jnp.zeros((rows, LANES), jnp.float32)] * 2
        for slot in range(capacity):
            word = word_ref[number, slot]
            first = scale_ref[number, slot + 2 * capacity]
            second = scale_ref[number, slot + 3 * capacity]
            base = word >> (LANES.bit_length() - 1)
            shift = word & (LANES - 1)
            stays = left >= shift
            one_kind = jnp.where(
                stays, trace_ref[pl.ds(base + 1, rows), :], trace_ref[pl.ds(base, rows), :]
            )
            base = base + 2 * rows
            other_kind = jnp.where(
                stays, trace_ref[pl.ds(base + 1, rows), :], trace_ref[pl.ds(base, rows), :]
            )
            moved = pltpu.roll(one_kind * first + other_kind * second, shift, 1)
            total[slot % 2] = total[slot % 2] + moved
        out_ref[number] = total[0] + total[1]


def smooth_kernel(rates_ref, part_ref, out_ref):
    signal = jnp.sum(part_ref[...], axis=0)
    taps = rates_ref.shape[0]
    rows = signal.shape[0]
    row = lax.broadcasted_iota(jnp.int32, (rows, LANES), 0)
    lane = lax.broadcasted_iota(jnp.int32, (rows, LANES), 1)
    previous = jnp.where(row == 0, 0.0, pltpu.roll(signal, 1, 0))
    total = [jnp.zeros_like(signal)] * 4
    for tap in range(taps):
        moved = signal
        if tap > 0:
            moved = pltpu.roll(jnp.where(lane < LANES - tap, signal, previous), tap, 1)
        total[tap % 4] = total[tap % 4] + moved * rates_ref[tap : tap + 1, :]
    out_ref[...] = (total[0] + total[1]) + (total[2] + total[3])


def local(
    green_tensor,
    mechanism,
    point_owner,
    point_row,
    onset_step,
    slip_amount,
    point_count,
    rake_angle,
    slip_rate,
):
    owners = lax.axis_size("owner")
    variations, length = point_row.shape
    points, parts, steps = green_tensor.shape
    taps = slip_rate.shape[1]
    rows = steps // LANES
    capacity = 2 * length // owners
    assert variations == 1 and capacity * FIELDS <= LANES
    listed = [point_owner.reshape(1, length), point_row, onset_step, slip_amount]
    table = pl.pallas_call(
        functools.partial(route_kernel, capacity, rows),
        out_shape=jax.ShapeDtypeStruct((owners, LANES), jnp.float32),
        in_specs=[SMEM] * 2 + [ANY] * 4,
        out_specs=VMEM,
        scratch_shapes=[pltpu.VMEM((1, length), array.dtype) for array in listed]
        + [pltpu.SemaphoreType.DMA((4,))],
        compiler_params=SMALL,
        name="route",
    )(point_count, rake_angle, *[in_hbm(array) for array in listed])
    table = lax.all_to_all(
        table.reshape(owners, 1, LANES), "owner", split_axis=0, concat_axis=0, tiled=True
    )
    group, chunk = 16, 32
    traces, rates = pl.pallas_call(
        functools.partial(project_kernel, rows, group, chunk),
        out_shape=(
            pltpu.VMEM((points * 4 * rows, LANES), jnp.float32),
            pltpu.VMEM((taps, LANES), jnp.float32),
        ),
        in_specs=[ANY] * 3,
        out_specs=(VMEM, VMEM),
        scratch_shapes=[
            pltpu.VMEM((parts, 2, points), jnp.float32),
            pltpu.VMEM((1, taps), jnp.float32),
            pltpu.VMEM((parts, points, steps), jnp.bfloat16),
            pltpu.VMEM((LANES, points), jnp.float32),
            pltpu.VMEM((points, LANES), jnp.float32),
            pltpu.SemaphoreType.DMA((2,)),
            pltpu.SemaphoreType.DMA((points // chunk,)),
        ],
        compiler_params=SMALL,
        name="project",
    )(
        in_hbm(jnp.transpose(mechanism, (1, 0, 2))),
        in_hbm(slip_rate),
        in_hbm(jnp.transpose(green_tensor, (1, 0, 2))),
    )
    partial = pl.pallas_call(
        functools.partial(gather_kernel, capacity, rows),
        out_shape=pltpu.VMEM((owners, rows, LANES), jnp.float32),
        in_specs=[VMEM, VMEM],
        out_specs=VMEM,
        scratch_shapes=[
            pltpu.VMEM((owners, LANES), jnp.int32),
            pltpu.SMEM((owners, LANES), jnp.int32),
            pltpu.SMEM((owners, LANES), jnp.float32),
            pltpu.SemaphoreType.DMA((2,)),
        ],
        compiler_params=SMALL,
        name="gather",
    )(in_vmem(table.reshape(owners, LANES)), in_vmem(traces))
    partial = lax.all_to_all(partial, "owner", split_axis=0, concat_axis=0, tiled=True)
    result = pl.pallas_call(
        smooth_kernel,
        out_shape=jax.ShapeDtypeStruct((rows, LANES), jnp.float32),
        in_specs=[VMEM, VMEM],
        out_specs=VMEM,
        compiler_params=SMALL,
        name="smooth",
    )(in_vmem(rates), in_vmem(partial))
    return result.reshape(1, steps)


def solution(mesh):
    in_specs = (
        P(("site", "owner"), None, None),
        P(None, None, "owner"),
        P("owner", None, None),
        P("owner", None),
        P("owner", None),
        P("owner", None),
        P("owner"),
        P("owner"),
        P("owner", None),
    )
    out_specs = P(("site", "owner"), None)
    return jax.shard_map(local, mesh=mesh, in_specs=in_specs, out_specs=out_specs, check_vma=False)
```

```python
import functools

import jax
import jax.numpy as jnp
from jax import lax
from jax.experimental import pallas as pl
from jax.experimental.pallas import tpu as pltpu
from jax.sharding import PartitionSpec as P

LANES = 128
FIELDS = 4
ANY = pl.BlockSpec(memory_space=pltpu.HBM)
SMEM = pl.BlockSpec(memory_space=pltpu.SMEM)
VMEM = pl.BlockSpec(memory_space=pltpu.VMEM)
SMALL = pltpu.CompilerParams(vmem_limit_bytes=16 << 20)


def in_hbm(array):
    return pltpu.with_memory_space_constraint(array, pltpu.HBM)


def in_vmem(array):
    return pltpu.with_memory_space_constraint(array, pltpu.VMEM)


def fetch(sources, targets, arrived):
    copies = [
        pltpu.make_async_copy(source, target, arrived.at[number])
        for number, (source, target) in enumerate(zip(sources, targets))
    ]
    for copy in copies:
        copy.start()
    for copy in copies:
        copy.wait()


def route_kernel(capacity, rows, *refs):
    count_ref, rake_ref, sources, out_ref, targets, arrived = (
        refs[0], refs[1], refs[2:6], refs[6], refs[7:11], refs[11]
    )
    fetch(sources, targets, arrived)
    owner_ref, row_ref, onset_ref, slip_ref = targets
    owners = out_ref.shape[0]
    length = row_ref.shape[1]
    lane = lax.broadcasted_iota(jnp.int32, (1, length), 1)
    alive = lane < count_ref[0]
    owner_index = lax.broadcasted_iota(jnp.int32, (owners, length), 0)
    hot = ((owner_index == owner_ref[...]) & alive).astype(jnp.float32)
    earlier = lax.broadcasted_iota(jnp.int32, (length, length), 0) < lax.broadcasted_iota(
        jnp.int32, (length, length), 1
    )
    before = jnp.dot(
        hot.astype(jnp.bfloat16), earlier.astype(jnp.bfloat16), preferred_element_type=jnp.float32
    )
    rank = jnp.sum(hot * before, axis=0, keepdims=True).astype(jnp.int32)
    onset = onset_ref[...]
    whole = onset >> (LANES.bit_length() - 1)
    base = row_ref[...] * (4 * rows) + (rows - 1) - whole
    rake = jnp.full((1, length), rake_ref[0], jnp.float32)
    weight = jnp.where(alive, slip_ref[...], 0.0)
    fields = (
        base.astype(jnp.float32),
        (onset & (LANES - 1)).astype(jnp.float32),
        jnp.cos(rake) * weight,
        jnp.sin(rake) * weight,
    )
    place = lax.broadcasted_iota(jnp.int32, (len(fields) * capacity, length), 0)
    pieces = []
    for field in fields:
        piece = []
        for _ in range(3):
            piece.append(field.astype(jnp.bfloat16).astype(jnp.float32))
            field = field - piece[-1]
        pieces.append(piece)
    total = None
    for part in range(3):
        spread = jnp.zeros(place.shape, jnp.float32)
        for number, piece in enumerate(pieces):
            spread = jnp.where(place == rank + number * capacity, piece[part], spread)
        term = lax.dot_general(
            hot.astype(jnp.bfloat16),
            spread.astype(jnp.bfloat16),
            (((1,), (1,)), ((), ())),
            preferred_element_type=jnp.float32,
        )
        total = term if part == 0 else total + term
    out_ref[...] = jnp.zeros_like(out_ref)
    out_ref[:, 0 : total.shape[1]] = total


def project_kernel(
    rows, group, chunk, mech_ref, rate_ref, green_ref, out_ref, rates_ref,
    mech_here, rate_here, green_here, flat_ref, column_ref, arrived, landed,
):
    parts, points, _ = green_ref.shape
    small = [
        pltpu.make_async_copy(mech_ref, mech_here, arrived.at[0]),
        pltpu.make_async_copy(rate_ref, rate_here, arrived.at[1]),
    ]
    large = [
        pltpu.make_async_copy(
            green_ref.at[:, pl.ds(first, chunk), :], green_here.at[:, pl.ds(first, chunk), :], landed.at[number]
        )
        for number, first in enumerate(range(0, points, chunk))
    ]
    for copy in small + large:
        copy.start()
    blank = jnp.zeros((rows, LANES), jnp.float32)

    def clear(number, carry):
        out_ref[pl.ds(pl.multiple_of(number * 2 * rows, rows), rows), :] = blank
        return carry

    lax.fori_loop(0, 2 * points, clear, 0, unroll=8)
    flat_ref[...] = jnp.zeros_like(flat_ref)
    for copy in small:
        copy.wait()
    taps = rate_here.shape[1]
    for part in range(parts):
        for kind in range(2):
            flat_ref[2 * part + kind : 2 * part + kind + 1, :] = mech_here[part, kind : kind + 1, :]
    flat_ref[2 * parts : 2 * parts + 1, 0:taps] = rate_here[...]
    column_ref[...] = flat_ref[...].T
    rates_ref[...] = jnp.broadcast_to(column_ref[0:taps, 2 * parts : 2 * parts + 1], (taps, LANES))

    def one(number, carry):
        first = pl.multiple_of(number * group, group)
        scale = [
            jnp.broadcast_to(column_ref[pl.ds(first, group), i : i + 1], (group, LANES))
            for i in range(2 * parts)
        ]
        for step in range(rows):
            total = [jnp.zeros((group, LANES), jnp.float32)] * 2
            for part in range(parts):
                block = green_here[part, pl.ds(first, group), step * LANES : (step + 1) * LANES].astype(
                    jnp.float32
                )
                total = [total[kind] + scale[2 * part + kind] * block for kind in range(2)]
            for kind in range(2):
                kept = total[kind].astype(jnp.bfloat16).astype(jnp.float32)
                for half in range(group // 8):
                    start = (first + half * 8) * (4 * rows) + kind * 2 * rows + rows + step
                    out_ref[pl.ds(start, 8, stride=4 * rows), :] = kept[half * 8 : half * 8 + 8]
        return carry

    for number, copy in enumerate(large):
        copy.wait()
        lax.fori_loop(number * (chunk // group), (number + 1) * (chunk // group), one, 0)


def gather_kernel(capacity, rows, sent_ref, trace_ref, out_ref, word_here, word_ref, scale_ref, arrived):
    scales = pltpu.make_async_copy(sent_ref, scale_ref, arrived.at[0])
    scales.start()
    word_here[...] = (sent_ref[...] + 0.5).astype(jnp.int32)
    words = pltpu.make_async_copy(word_here, word_ref, arrived.at[1])
    words.start()
    left = LANES - 1 - lax.broadcasted_iota(jnp.int32, (rows, LANES), 1)
    scales.wait()
    words.wait()
    for number in range(out_ref.shape[0]):
        total = [jnp.zeros((rows, LANES), jnp.float32)] * 2
        for slot in range(capacity):
            base = word_ref[number, slot]
            shift = word_ref[number, slot + capacity]
            first = scale_ref[number, slot + 2 * capacity]
            second = scale_ref[number, slot + 3 * capacity]
            stays = left >= shift
            one_kind = jnp.where(
                stays, trace_ref[pl.ds(base + 1, rows), :], trace_ref[pl.ds(base, rows), :]
            )
            base = base + 2 * rows
            other_kind = jnp.where(
                stays, trace_ref[pl.ds(base + 1, rows), :], trace_ref[pl.ds(base, rows), :]
            )
            moved = pltpu.roll(one_kind * first + other_kind * second, shift, 1)
            total[slot % 2] = total[slot % 2] + moved
        out_ref[number] = total[0] + total[1]


def smooth_kernel(rates_ref, part_ref, out_ref):
    signal = jnp.sum(part_ref[...], axis=0)
    taps = rates_ref.shape[0]
    rows = signal.shape[0]
    row = lax.broadcasted_iota(jnp.int32, (rows, LANES), 0)
    lane = lax.broadcasted_iota(jnp.int32, (rows, LANES), 1)
    previous = jnp.where(row == 0, 0.0, pltpu.roll(signal, 1, 0))
    total = [jnp.zeros_like(signal)] * 4
    for tap in range(taps):
        moved = signal
        if tap > 0:
            moved = pltpu.roll(jnp.where(lane < LANES - tap, signal, previous), tap, 1)
        total[tap % 4] = total[tap % 4] + moved * rates_ref[tap : tap + 1, :]
    out_ref[...] = (total[0] + total[1]) + (total[2] + total[3])


def local(
    green_tensor,
    mechanism,
    point_owner,
    point_row,
    onset_step,
    slip_amount,
    point_count,
    rake_angle,
    slip_rate,
):
    owners = lax.axis_size("owner")
    variations, length = point_row.shape
    points, parts, steps = green_tensor.shape
    taps = slip_rate.shape[1]
    rows = steps // LANES
    capacity = 2 * length // owners
    assert variations == 1 and capacity * FIELDS <= LANES
    listed = [point_owner.reshape(1, length), point_row, onset_step, slip_amount]
    table = pl.pallas_call(
        functools.partial(route_kernel, capacity, rows),
        out_shape=jax.ShapeDtypeStruct((owners, LANES), jnp.float32),
        in_specs=[SMEM] * 2 + [ANY] * 4,
        out_specs=VMEM,
        scratch_shapes=[pltpu.VMEM((1, length), array.dtype) for array in listed]
        + [pltpu.SemaphoreType.DMA((4,))],
        compiler_params=SMALL,
        name="route",
    )(point_count, rake_angle, *[in_hbm(array) for array in listed])
    table = lax.all_to_all(
        table.reshape(owners, 1, LANES), "owner", split_axis=0, concat_axis=0, tiled=True
    )
    group, chunk = 16, 32
    traces, rates = pl.pallas_call(
        functools.partial(project_kernel, rows, group, chunk),
        out_shape=(
            pltpu.VMEM((points * 4 * rows, LANES), jnp.float32),
            pltpu.VMEM((taps, LANES), jnp.float32),
        ),
        in_specs=[ANY] * 3,
        out_specs=(VMEM, VMEM),
        scratch_shapes=[
            pltpu.VMEM((parts, 2, points), jnp.float32),
            pltpu.VMEM((1, taps), jnp.float32),
            pltpu.VMEM((parts, points, steps), jnp.bfloat16),
            pltpu.VMEM((LANES, points), jnp.float32),
            pltpu.VMEM((points, LANES), jnp.float32),
            pltpu.SemaphoreType.DMA((2,)),
            pltpu.SemaphoreType.DMA((points // chunk,)),
        ],
        compiler_params=SMALL,
        name="project",
    )(
        in_hbm(jnp.transpose(mechanism, (1, 0, 2))),
        in_hbm(slip_rate),
        in_hbm(jnp.transpose(green_tensor, (1, 0, 2))),
    )
    partial = pl.pallas_call(
        functools.partial(gather_kernel, capacity, rows),
        out_shape=pltpu.VMEM((owners, rows, LANES), jnp.float32),
        in_specs=[VMEM, VMEM],
        out_specs=VMEM,
        scratch_shapes=[
            pltpu.VMEM((owners, LANES), jnp.int32),
            pltpu.SMEM((owners, LANES), jnp.int32),
            pltpu.SMEM((owners, LANES), jnp.float32),
            pltpu.SemaphoreType.DMA((2,)),
        ],
        compiler_params=SMALL,
        name="gather",
    )(in_vmem(table.reshape(owners, LANES)), in_vmem(traces))
    partial = lax.all_to_all(partial, "owner", split_axis=0, concat_axis=0, tiled=True)
    result = pl.pallas_call(
        smooth_kernel,
        out_shape=jax.ShapeDtypeStruct((rows, LANES), jnp.float32),
        in_specs=[VMEM, VMEM],
        out_specs=VMEM,
        compiler_params=SMALL,
        name="smooth",
    )(in_vmem(rates), in_vmem(partial))
    return result.reshape(1, steps)


def solution(mesh):
    in_specs = (
        P(("site", "owner"), None, None),
        P(None, None, "owner"),
        P("owner", None, None),
        P("owner", None),
        P("owner", None),
        P("owner", None),
        P("owner"),
        P("owner"),
        P("owner", None),
    )
    out_specs = P(("site", "owner"), None)
    return jax.shard_map(local, mesh=mesh, in_specs=in_specs, out_specs=out_specs, check_vma=False)
```

```python
import functools

import jax
import jax.numpy as jnp
from jax import lax
from jax.experimental import pallas as pl
from jax.experimental.pallas import tpu as pltpu
from jax.sharding import PartitionSpec as P

LANES = 128
FIELDS = 4
ANY = pl.BlockSpec(memory_space=pltpu.HBM)
SMEM = pl.BlockSpec(memory_space=pltpu.SMEM)
VMEM = pl.BlockSpec(memory_space=pltpu.VMEM)
SMALL = pltpu.CompilerParams(vmem_limit_bytes=16 << 20)


def in_hbm(array):
    return pltpu.with_memory_space_constraint(array, pltpu.HBM)


def in_vmem(array):
    return pltpu.with_memory_space_constraint(array, pltpu.VMEM)


def fetch(sources, targets, arrived):
    copies = [
        pltpu.make_async_copy(source, target, arrived.at[number])
        for number, (source, target) in enumerate(zip(sources, targets))
    ]
    for copy in copies:
        copy.start()
    for copy in copies:
        copy.wait()


def route_kernel(capacity, rows, *refs):
    count_ref, rake_ref, sources, out_ref, targets, arrived = (
        refs[0], refs[1], refs[2:6], refs[6], refs[7:11], refs[11]
    )
    fetch(sources, targets, arrived)
    owner_ref, row_ref, onset_ref, slip_ref = targets
    owners = out_ref.shape[0]
    length = row_ref.shape[1]
    lane = lax.broadcasted_iota(jnp.int32, (1, length), 1)
    alive = lane < count_ref[0]
    owner_index = lax.broadcasted_iota(jnp.int32, (owners, length), 0)
    hot = ((owner_index == owner_ref[...]) & alive).astype(jnp.float32)
    earlier = lax.broadcasted_iota(jnp.int32, (length, length), 0) < lax.broadcasted_iota(
        jnp.int32, (length, length), 1
    )
    before = jnp.dot(
        hot.astype(jnp.bfloat16), earlier.astype(jnp.bfloat16), preferred_element_type=jnp.float32
    )
    rank = jnp.sum(hot * before, axis=0, keepdims=True).astype(jnp.int32)
    onset = onset_ref[...]
    whole = onset >> (LANES.bit_length() - 1)
    base = row_ref[...] * (4 * rows + 1) + (rows - 1) - whole
    rake = jnp.full((1, length), rake_ref[0], jnp.float32)
    weight = jnp.where(alive, slip_ref[...], 0.0)
    fields = (
        base.astype(jnp.float32),
        (onset & (LANES - 1)).astype(jnp.float32),
        jnp.cos(rake) * weight,
        jnp.sin(rake) * weight,
    )
    place = lax.broadcasted_iota(jnp.int32, (len(fields) * capacity, length), 0)
    pieces = []
    for field in fields:
        piece = []
        for _ in range(3):
            piece.append(field.astype(jnp.bfloat16).astype(jnp.float32))
            field = field - piece[-1]
        pieces.append(piece)
    total = None
    for part in range(3):
        spread = jnp.zeros(place.shape, jnp.float32)
        for number, piece in enumerate(pieces):
            spread = jnp.where(place == rank + number * capacity, piece[part], spread)
        term = lax.dot_general(
            hot.astype(jnp.bfloat16),
            spread.astype(jnp.bfloat16),
            (((1,), (1,)), ((), ())),
            preferred_element_type=jnp.float32,
        )
        total = term if part == 0 else total + term
    out_ref[...] = jnp.zeros_like(out_ref)
    out_ref[:, 0 : total.shape[1]] = total


def project_kernel(
    rows, group, chunk, mech_ref, rate_ref, green_ref, out_ref, rates_ref,
    mech_here, rate_here, green_here, flat_ref, column_ref, arrived, landed,
):
    parts, points, _ = green_ref.shape
    small = [
        pltpu.make_async_copy(mech_ref, mech_here, arrived.at[0]),
        pltpu.make_async_copy(rate_ref, rate_here, arrived.at[1]),
    ]
    large = [
        pltpu.make_async_copy(
            green_ref.at[:, pl.ds(first, chunk), :], green_here.at[:, pl.ds(first, chunk), :], landed.at[number]
        )
        for number, first in enumerate(range(0, points, chunk))
    ]
    for copy in small + large:
        copy.start()
    pitch = 4 * rows + 1
    blank = jnp.zeros((rows, LANES), jnp.float32)

    def clear(number, carry):
        for kind in range(2):
            out_ref[pl.ds(number * pitch + kind * 2 * rows, rows), :] = blank
        return carry

    lax.fori_loop(0, points, clear, 0, unroll=8)
    flat_ref[...] = jnp.zeros_like(flat_ref)
    for copy in small:
        copy.wait()
    taps = rate_here.shape[1]
    for part in range(parts):
        for kind in range(2):
            flat_ref[2 * part + kind : 2 * part + kind + 1, :] = mech_here[part, kind : kind + 1, :]
    flat_ref[2 * parts : 2 * parts + 1, 0:taps] = rate_here[...]
    column_ref[...] = flat_ref[...].T
    rates_ref[...] = jnp.broadcast_to(column_ref[0:taps, 2 * parts : 2 * parts + 1], (taps, LANES))

    def one(number, carry):
        first = pl.multiple_of(number * group, group)
        for half in range(0, group, 8):
            corner = (first + half) * pitch + rows
            scale = [
                jnp.broadcast_to(column_ref[pl.ds(first + half, 8), i : i + 1], (8, LANES))
                for i in range(2 * parts)
            ]
            for step in range(rows):
                total = [None, None]
                for part in range(parts):
                    block = green_here[part, pl.ds(first, group), step * LANES : (step + 1) * LANES]
                    block = block.astype(jnp.float32)[half : half + 8]
                    for kind in range(2):
                        term = scale[2 * part + kind] * block
                        total[kind] = term if part == 0 else total[kind] + term
                for kind in range(2):
                    kept = total[kind].astype(jnp.bfloat16).astype(jnp.float32)
                    out_ref[pl.ds(corner + 2 * kind * rows + step, 8, stride=pitch), :] = kept
        return carry

    for number, copy in enumerate(large):
        copy.wait()
        lax.fori_loop(number * (chunk // group), (number + 1) * (chunk // group), one, 0)


def gather_kernel(capacity, rows, sent_ref, trace_ref, out_ref, word_here, word_ref, scale_ref, arrived):
    scales = pltpu.make_async_copy(sent_ref, scale_ref, arrived.at[0])
    scales.start()
    word_here[...] = (sent_ref[...] + 0.5).astype(jnp.int32)
    words = pltpu.make_async_copy(word_here, word_ref, arrived.at[1])
    words.start()
    left = LANES - 1 - lax.broadcasted_iota(jnp.int32, (rows, LANES), 1)
    scales.wait()
    words.wait()
    for number in range(out_ref.shape[0]):
        total = [jnp.zeros((rows, LANES), jnp.float32)] * 2
        for slot in range(capacity):
            base = word_ref[number, slot]
            shift = word_ref[number, slot + capacity]
            first = scale_ref[number, slot + 2 * capacity]
            second = scale_ref[number, slot + 3 * capacity]
            stays = left >= shift
            one_kind = jnp.where(
                stays, trace_ref[pl.ds(base + 1, rows), :], trace_ref[pl.ds(base, rows), :]
            )
            base = base + 2 * rows
            other_kind = jnp.where(
                stays, trace_ref[pl.ds(base + 1, rows), :], trace_ref[pl.ds(base, rows), :]
            )
            moved = pltpu.roll(one_kind * first + other_kind * second, shift, 1)
            total[slot % 2] = total[slot % 2] + moved
        out_ref[number] = total[0] + total[1]


def smooth_kernel(rates_ref, part_ref, out_ref):
    signal = jnp.sum(part_ref[...], axis=0)
    taps = rates_ref.shape[0]
    rows = signal.shape[0]
    row = lax.broadcasted_iota(jnp.int32, (rows, LANES), 0)
    lane = lax.broadcasted_iota(jnp.int32, (rows, LANES), 1)
    previous = jnp.where(row == 0, 0.0, pltpu.roll(signal, 1, 0))
    total = [jnp.zeros_like(signal)] * 4
    for tap in range(taps):
        moved = signal
        if tap > 0:
            moved = pltpu.roll(jnp.where(lane < LANES - tap, signal, previous), tap, 1)
        total[tap % 4] = total[tap % 4] + moved * rates_ref[tap : tap + 1, :]
    out_ref[...] = (total[0] + total[1]) + (total[2] + total[3])


def local(
    green_tensor,
    mechanism,
    point_owner,
    point_row,
    onset_step,
    slip_amount,
    point_count,
    rake_angle,
    slip_rate,
):
    owners = lax.axis_size("owner")
    variations, length = point_row.shape
    points, parts, steps = green_tensor.shape
    taps = slip_rate.shape[1]
    rows = steps // LANES
    capacity = 2 * length // owners
    assert variations == 1 and capacity * FIELDS <= LANES
    listed = [point_owner.reshape(1, length), point_row, onset_step, slip_amount]
    table = pl.pallas_call(
        functools.partial(route_kernel, capacity, rows),
        out_shape=jax.ShapeDtypeStruct((owners, LANES), jnp.float32),
        in_specs=[SMEM] * 2 + [ANY] * 4,
        out_specs=VMEM,
        scratch_shapes=[pltpu.VMEM((1, length), array.dtype) for array in listed]
        + [pltpu.SemaphoreType.DMA((4,))],
        compiler_params=SMALL,
        name="route",
    )(point_count, rake_angle, *[in_hbm(array) for array in listed])
    table = lax.all_to_all(
        table.reshape(owners, 1, LANES), "owner", split_axis=0, concat_axis=0, tiled=True
    )
    group, chunk = 16, 32
    traces, rates = pl.pallas_call(
        functools.partial(project_kernel, rows, group, chunk),
        out_shape=(
            pltpu.VMEM((points * (4 * rows + 1), LANES), jnp.float32),
            pltpu.VMEM((taps, LANES), jnp.float32),
        ),
        in_specs=[ANY] * 3,
        out_specs=(VMEM, VMEM),
        scratch_shapes=[
            pltpu.VMEM((parts, 2, points), jnp.float32),
            pltpu.VMEM((1, taps), jnp.float32),
            pltpu.VMEM((parts, points, steps), jnp.bfloat16),
            pltpu.VMEM((LANES, points), jnp.float32),
            pltpu.VMEM((points, LANES), jnp.float32),
            pltpu.SemaphoreType.DMA((2,)),
            pltpu.SemaphoreType.DMA((points // chunk,)),
        ],
        compiler_params=SMALL,
        name="project",
    )(
        in_hbm(jnp.transpose(mechanism, (1, 0, 2))),
        in_hbm(slip_rate),
        in_hbm(jnp.transpose(green_tensor, (1, 0, 2))),
    )
    partial = pl.pallas_call(
        functools.partial(gather_kernel, capacity, rows),
        out_shape=pltpu.VMEM((owners, rows, LANES), jnp.float32),
        in_specs=[VMEM, VMEM],
        out_specs=VMEM,
        scratch_shapes=[
            pltpu.VMEM((owners, LANES), jnp.int32),
            pltpu.SMEM((owners, LANES), jnp.int32),
            pltpu.SMEM((owners, LANES), jnp.float32),
            pltpu.SemaphoreType.DMA((2,)),
        ],
        compiler_params=SMALL,
        name="gather",
    )(in_vmem(table.reshape(owners, LANES)), in_vmem(traces))
    partial = lax.all_to_all(partial, "owner", split_axis=0, concat_axis=0, tiled=True)
    result = pl.pallas_call(
        smooth_kernel,
        out_shape=jax.ShapeDtypeStruct((rows, LANES), jnp.float32),
        in_specs=[VMEM, VMEM],
        out_specs=VMEM,
        compiler_params=SMALL,
        name="smooth",
    )(in_vmem(rates), in_vmem(partial))
    return result.reshape(1, steps)


def solution(mesh):
    in_specs = (
        P(("site", "owner"), None, None),
        P(None, None, "owner"),
        P("owner", None, None),
        P("owner", None),
        P("owner", None),
        P("owner", None),
        P("owner"),
        P("owner"),
        P("owner", None),
    )
    out_specs = P(("site", "owner"), None)
    return jax.shard_map(local, mesh=mesh, in_specs=in_specs, out_specs=out_specs, check_vma=False)
```

```python
import functools

import jax
import jax.numpy as jnp
from jax import lax
from jax.experimental import pallas as pl
from jax.experimental.pallas import tpu as pltpu
from jax.sharding import PartitionSpec as P

LANES = 128
FIELDS = 4
ANY = pl.BlockSpec(memory_space=pltpu.HBM)
SMEM = pl.BlockSpec(memory_space=pltpu.SMEM)
VMEM = pl.BlockSpec(memory_space=pltpu.VMEM)
SMALL = pltpu.CompilerParams(vmem_limit_bytes=16 << 20)


def in_hbm(array):
    return pltpu.with_memory_space_constraint(array, pltpu.HBM)


def in_vmem(array):
    return pltpu.with_memory_space_constraint(array, pltpu.VMEM)


def route_kernel(capacity, rows, *refs):
    count_ref, rake_ref, sources, out_ref, targets, arrived = (
        refs[0], refs[1], refs[2:6], refs[6], refs[7:11], refs[11]
    )
    turn_ref, earlier_ref = refs[12:]
    copies = [
        pltpu.make_async_copy(source, target, arrived.at[number])
        for number, (source, target) in enumerate(zip(sources, targets))
    ]
    for copy in copies:
        copy.start()
    owner_ref, row_ref, onset_ref, slip_ref = targets
    owners = out_ref.shape[0]
    length = row_ref.shape[1]
    out_ref[...] = jnp.zeros_like(out_ref)
    alive = lax.broadcasted_iota(jnp.int32, (1, length), 1) < count_ref[0]
    rake = jnp.full((1, length), rake_ref[0], jnp.float32)
    turn_ref[0:1, :] = jnp.where(alive, jnp.cos(rake), 0.0)
    turn_ref[1:2, :] = jnp.where(alive, jnp.sin(rake), 0.0)
    earlier = lax.broadcasted_iota(jnp.int32, (length, length), 0) < lax.broadcasted_iota(
        jnp.int32, (length, length), 1
    )
    earlier_ref[...] = earlier.astype(jnp.float32).astype(jnp.bfloat16)
    for copy in copies:
        copy.wait()
    owner_index = lax.broadcasted_iota(jnp.int32, (owners, length), 0)
    hot = ((owner_index == owner_ref[...]) & alive).astype(jnp.float32)
    before = jnp.dot(hot.astype(jnp.bfloat16), earlier_ref[...], preferred_element_type=jnp.float32)
    rank = jnp.sum(hot * before, axis=0, keepdims=True).astype(jnp.int32)
    onset = onset_ref[...]
    base = row_ref[...] * (4 * rows + 1) + (rows - 1) - (onset >> (LANES.bit_length() - 1))
    fields = (
        base.astype(jnp.float32),
        (onset & (LANES - 1)).astype(jnp.float32),
        turn_ref[0:1, :] * slip_ref[...],
        turn_ref[1:2, :] * slip_ref[...],
    )
    place = lax.broadcasted_iota(jnp.int32, (len(fields) * capacity, length), 0)
    pieces = []
    for field in fields:
        piece = []
        for _ in range(3):
            piece.append(field.astype(jnp.bfloat16).astype(jnp.float32))
            field = field - piece[-1]
        pieces.append(piece)
    total = None
    for part in range(3):
        spread = jnp.zeros(place.shape, jnp.float32)
        for number, piece in enumerate(pieces):
            spread = jnp.where(place == rank + number * capacity, piece[part], spread)
        term = lax.dot_general(
            hot.astype(jnp.bfloat16),
            spread.astype(jnp.bfloat16),
            (((1,), (1,)), ((), ())),
            preferred_element_type=jnp.float32,
        )
        total = term if part == 0 else total + term
    out_ref[:, 0 : total.shape[1]] = total


def project_kernel(
    rows, group, chunk, mech_ref, rate_ref, green_ref, out_ref, rates_ref,
    mech_here, rate_here, green_here, flat_ref, column_ref, arrived, landed,
):
    parts, points, _ = green_ref.shape
    small = [
        pltpu.make_async_copy(mech_ref, mech_here, arrived.at[0]),
        pltpu.make_async_copy(rate_ref, rate_here, arrived.at[1]),
    ]
    large = [
        pltpu.make_async_copy(
            green_ref.at[:, pl.ds(first, chunk), :], green_here.at[:, pl.ds(first, chunk), :], landed.at[number]
        )
        for number, first in enumerate(range(0, points, chunk))
    ]
    for copy in small + large:
        copy.start()
    pitch = 4 * rows + 1
    blank = jnp.zeros((rows, LANES), jnp.float32)

    def clear(number, carry):
        for kind in range(2):
            out_ref[pl.ds(number * pitch + kind * 2 * rows, rows), :] = blank
        return carry

    lax.fori_loop(0, points, clear, 0, unroll=8)
    flat_ref[...] = jnp.zeros_like(flat_ref)
    for copy in small:
        copy.wait()
    taps = rate_here.shape[1]
    for part in range(parts):
        for kind in range(2):
            flat_ref[2 * part + kind : 2 * part + kind + 1, :] = mech_here[part, kind : kind + 1, :]
    flat_ref[2 * parts : 2 * parts + 1, 0:taps] = rate_here[...]
    column_ref[...] = flat_ref[...].T
    rates_ref[...] = jnp.broadcast_to(column_ref[0:taps, 2 * parts : 2 * parts + 1], (taps, LANES))

    def one(number, carry):
        first = pl.multiple_of(number * group, group)
        for half in range(0, group, 8):
            corner = (first + half) * pitch + rows
            scale = [
                jnp.broadcast_to(column_ref[pl.ds(first + half, 8), i : i + 1], (8, LANES))
                for i in range(2 * parts)
            ]
            for step in range(rows):
                total = [None, None]
                for part in range(parts):
                    block = green_here[part, pl.ds(first, group), step * LANES : (step + 1) * LANES]
                    block = block.astype(jnp.float32)[half : half + 8]
                    for kind in range(2):
                        term = scale[2 * part + kind] * block
                        total[kind] = term if part == 0 else total[kind] + term
                for kind in range(2):
                    kept = total[kind].astype(jnp.bfloat16).astype(jnp.float32)
                    out_ref[pl.ds(corner + 2 * kind * rows + step, 8, stride=pitch), :] = kept
        return carry

    for number, copy in enumerate(large):
        copy.wait()
        lax.fori_loop(number * (chunk // group), (number + 1) * (chunk // group), one, 0)


def gather_kernel(capacity, rows, sent_ref, trace_ref, out_ref, word_here, word_ref, scale_ref, arrived):
    scales = pltpu.make_async_copy(sent_ref, scale_ref, arrived.at[0])
    scales.start()
    word_here[...] = (sent_ref[...] + 0.5).astype(jnp.int32)
    words = pltpu.make_async_copy(word_here, word_ref, arrived.at[1])
    words.start()
    left = LANES - 1 - lax.broadcasted_iota(jnp.int32, (rows, LANES), 1)
    scales.wait()
    words.wait()
    for number in range(out_ref.shape[0]):
        total = [jnp.zeros((rows, LANES), jnp.float32)] * 2
        for slot in range(capacity):
            base = word_ref[number, slot]
            shift = word_ref[number, slot + capacity]
            first = scale_ref[number, slot + 2 * capacity]
            second = scale_ref[number, slot + 3 * capacity]
            stays = left >= shift
            one_kind = jnp.where(
                stays, trace_ref[pl.ds(base + 1, rows), :], trace_ref[pl.ds(base, rows), :]
            )
            base = base + 2 * rows
            other_kind = jnp.where(
                stays, trace_ref[pl.ds(base + 1, rows), :], trace_ref[pl.ds(base, rows), :]
            )
            moved = pltpu.roll(one_kind * first + other_kind * second, shift, 1)
            total[slot % 2] = total[slot % 2] + moved
        out_ref[number] = total[0] + total[1]


def smooth_kernel(rates_ref, part_ref, out_ref):
    signal = jnp.sum(part_ref[...], axis=0)
    taps = rates_ref.shape[0]
    rows = signal.shape[0]
    row = lax.broadcasted_iota(jnp.int32, (rows, LANES), 0)
    lane = lax.broadcasted_iota(jnp.int32, (rows, LANES), 1)
    previous = jnp.where(row == 0, 0.0, pltpu.roll(signal, 1, 0))
    total = [jnp.zeros_like(signal)] * 4
    for tap in range(taps):
        moved = signal
        if tap > 0:
            moved = pltpu.roll(jnp.where(lane < LANES - tap, signal, previous), tap, 1)
        total[tap % 4] = total[tap % 4] + moved * rates_ref[tap : tap + 1, :]
    out_ref[...] = (total[0] + total[1]) + (total[2] + total[3])


def local(
    green_tensor,
    mechanism,
    point_owner,
    point_row,
    onset_step,
    slip_amount,
    point_count,
    rake_angle,
    slip_rate,
):
    owners = lax.axis_size("owner")
    variations, length = point_row.shape
    points, parts, steps = green_tensor.shape
    taps = slip_rate.shape[1]
    rows = steps // LANES
    capacity = 2 * length // owners
    assert variations == 1 and capacity * FIELDS <= LANES
    listed = [point_owner.reshape(1, length), point_row, onset_step, slip_amount]
    table = pl.pallas_call(
        functools.partial(route_kernel, capacity, rows),
        out_shape=jax.ShapeDtypeStruct((owners, LANES), jnp.float32),
        in_specs=[SMEM] * 2 + [ANY] * 4,
        out_specs=VMEM,
        scratch_shapes=[pltpu.VMEM((1, length), array.dtype) for array in listed]
        + [
            pltpu.SemaphoreType.DMA((4,)),
            pltpu.VMEM((2, length), jnp.float32),
            pltpu.VMEM((length, length), jnp.bfloat16),
        ],
        compiler_params=SMALL,
        name="route",
    )(point_count, rake_angle, *[in_hbm(array) for array in listed])
    table = lax.all_to_all(
        table.reshape(owners, 1, LANES), "owner", split_axis=0, concat_axis=0, tiled=True
    )
    group, chunk = 16, 32
    traces, rates = pl.pallas_call(
        functools.partial(project_kernel, rows, group, chunk),
        out_shape=(
            pltpu.VMEM((points * (4 * rows + 1), LANES), jnp.float32),
            pltpu.VMEM((taps, LANES), jnp.float32),
        ),
        in_specs=[ANY] * 3,
        out_specs=(VMEM, VMEM),
        scratch_shapes=[
            pltpu.VMEM((parts, 2, points), jnp.float32),
            pltpu.VMEM((1, taps), jnp.float32),
            pltpu.VMEM((parts, points, steps), jnp.bfloat16),
            pltpu.VMEM((LANES, points), jnp.float32),
            pltpu.VMEM((points, LANES), jnp.float32),
            pltpu.SemaphoreType.DMA((2,)),
            pltpu.SemaphoreType.DMA((points // chunk,)),
        ],
        compiler_params=SMALL,
        name="project",
    )(
        in_hbm(jnp.transpose(mechanism, (1, 0, 2))),
        in_hbm(slip_rate),
        in_hbm(jnp.transpose(green_tensor, (1, 0, 2))),
    )
    partial = pl.pallas_call(
        functools.partial(gather_kernel, capacity, rows),
        out_shape=pltpu.VMEM((owners, rows, LANES), jnp.float32),
        in_specs=[VMEM, VMEM],
        out_specs=VMEM,
        scratch_shapes=[
            pltpu.VMEM((owners, LANES), jnp.int32),
            pltpu.SMEM((owners, LANES), jnp.int32),
            pltpu.SMEM((owners, LANES), jnp.float32),
            pltpu.SemaphoreType.DMA((2,)),
        ],
        compiler_params=SMALL,
        name="gather",
    )(in_vmem(table.reshape(owners, LANES)), in_vmem(traces))
    partial = lax.all_to_all(partial, "owner", split_axis=0, concat_axis=0, tiled=True)
    result = pl.pallas_call(
        smooth_kernel,
        out_shape=jax.ShapeDtypeStruct((rows, LANES), jnp.float32),
        in_specs=[VMEM, VMEM],
        out_specs=VMEM,
        compiler_params=SMALL,
        name="smooth",
    )(in_vmem(rates), in_vmem(partial))
    return result.reshape(1, steps)


def solution(mesh):
    in_specs = (
        P(("site", "owner"), None, None),
        P(None, None, "owner"),
        P("owner", None, None),
        P("owner", None),
        P("owner", None),
        P("owner", None),
        P("owner"),
        P("owner"),
        P("owner", None),
    )
    out_specs = P(("site", "owner"), None)
    return jax.shard_map(local, mesh=mesh, in_specs=in_specs, out_specs=out_specs, check_vma=False)
```

```python
import functools

import jax
import jax.numpy as jnp
from jax import lax
from jax.experimental import pallas as pl
from jax.experimental.pallas import tpu as pltpu
from jax.sharding import PartitionSpec as P

LANES = 128
FIELDS = 4
ANY = pl.BlockSpec(memory_space=pltpu.HBM)
SMEM = pl.BlockSpec(memory_space=pltpu.SMEM)
VMEM = pl.BlockSpec(memory_space=pltpu.VMEM)
SMALL = pltpu.CompilerParams(vmem_limit_bytes=16 << 20)


def in_hbm(array):
    return pltpu.with_memory_space_constraint(array, pltpu.HBM)


def in_vmem(array):
    return pltpu.with_memory_space_constraint(array, pltpu.VMEM)


def fetch(sources, targets, arrived):
    copies = [
        pltpu.make_async_copy(source, target, arrived.at[number])
        for number, (source, target) in enumerate(zip(sources, targets))
    ]
    for copy in copies:
        copy.start()
    for copy in copies:
        copy.wait()


def route_kernel(capacity, rows, *refs):
    count_ref, rake_ref, sources, out_ref, targets, arrived = (
        refs[0], refs[1], refs[2:6], refs[6], refs[7:11], refs[11]
    )
    fetch(sources, targets, arrived)
    owner_ref, row_ref, onset_ref, slip_ref = targets
    owners = out_ref.shape[0]
    length = row_ref.shape[1]
    lane = lax.broadcasted_iota(jnp.int32, (1, length), 1)
    alive = lane < count_ref[0]
    owner_index = lax.broadcasted_iota(jnp.int32, (owners, length), 0)
    hot = ((owner_index == owner_ref[...]) & alive).astype(jnp.float32)
    earlier = lax.broadcasted_iota(jnp.int32, (length, length), 0) < lax.broadcasted_iota(
        jnp.int32, (length, length), 1
    )
    before = jnp.dot(
        hot.astype(jnp.bfloat16), earlier.astype(jnp.bfloat16), preferred_element_type=jnp.float32
    )
    rank = jnp.sum(hot * before, axis=0, keepdims=True).astype(jnp.int32)
    onset = onset_ref[...]
    whole = onset >> (LANES.bit_length() - 1)
    base = row_ref[...] * (4 * rows + 1) + (rows - 1) - whole
    rake = jnp.full((1, length), rake_ref[0], jnp.float32)
    weight = jnp.where(alive, slip_ref[...], 0.0)
    fields = (
        base.astype(jnp.float32),
        (onset & (LANES - 1)).astype(jnp.float32),
        jnp.cos(rake) * weight,
        jnp.sin(rake) * weight,
    )
    place = lax.broadcasted_iota(jnp.int32, (len(fields) * capacity, length), 0)
    pieces = []
    for field in fields:
        piece = []
        for _ in range(3):
            piece.append(field.astype(jnp.bfloat16).astype(jnp.float32))
            field = field - piece[-1]
        pieces.append(piece)
    total = None
    for part in range(3):
        spread = jnp.zeros(place.shape, jnp.float32)
        for number, piece in enumerate(pieces):
            spread = jnp.where(place == rank + number * capacity, piece[part], spread)
        term = lax.dot_general(
            hot.astype(jnp.bfloat16),
            spread.astype(jnp.bfloat16),
            (((1,), (1,)), ((), ())),
            preferred_element_type=jnp.float32,
        )
        total = term if part == 0 else total + term
    out_ref[...] = jnp.zeros_like(out_ref)
    out_ref[:, 0 : total.shape[1]] = total


def project_kernel(
    rows, group, chunk, mech_ref, rate_ref, green_ref, out_ref, rates_ref,
    mech_here, rate_here, green_here, flat_ref, column_ref, arrived, landed,
):
    parts, points, _ = green_ref.shape
    small = [
        pltpu.make_async_copy(mech_ref, mech_here, arrived.at[0]),
        pltpu.make_async_copy(rate_ref, rate_here, arrived.at[1]),
    ]
    large = [
        pltpu.make_async_copy(
            green_ref.at[:, pl.ds(first, chunk), :], green_here.at[:, pl.ds(first, chunk), :], landed.at[number]
        )
        for number, first in enumerate(range(0, points, chunk))
    ]
    for copy in small + large:
        copy.start()
    pitch = 4 * rows + 1
    blank = jnp.zeros((rows, LANES), jnp.float32)

    def clear(number, carry):
        for kind in range(2):
            out_ref[pl.ds(number * pitch + kind * 2 * rows, rows), :] = blank
        return carry

    lax.fori_loop(0, points, clear, 0, unroll=8)
    flat_ref[...] = jnp.zeros_like(flat_ref)
    for copy in small:
        copy.wait()
    taps = rate_here.shape[1]
    for part in range(parts):
        for kind in range(2):
            flat_ref[2 * part + kind : 2 * part + kind + 1, :] = mech_here[part, kind : kind + 1, :]
    flat_ref[2 * parts : 2 * parts + 1, 0:taps] = rate_here[...]
    column_ref[...] = flat_ref[...].T
    rates_ref[...] = jnp.broadcast_to(column_ref[0:taps, 2 * parts : 2 * parts + 1], (taps, LANES))

    def one(number, carry):
        first = pl.multiple_of(number * group, group)
        for half in range(0, group, 8):
            corner = (first + half) * pitch + rows
            scale = [
                jnp.broadcast_to(column_ref[pl.ds(first + half, 8), i : i + 1], (8, LANES))
                for i in range(2 * parts)
            ]
            for step in range(rows):
                total = [None, None]
                for part in range(parts):
                    block = green_here[part, pl.ds(first, group), step * LANES : (step + 1) * LANES]
                    block = block.astype(jnp.float32)[half : half + 8]
                    for kind in range(2):
                        term = scale[2 * part + kind] * block
                        total[kind] = term if part == 0 else total[kind] + term
                for kind in range(2):
                    kept = total[kind].astype(jnp.bfloat16).astype(jnp.float32)
                    out_ref[pl.ds(corner + 2 * kind * rows + step, 8, stride=pitch), :] = kept
        return carry

    for number, copy in enumerate(large):
        copy.wait()
        lax.fori_loop(number * (chunk // group), (number + 1) * (chunk // group), one, 0)


def gather_kernel(
    capacity, rows, sent_ref, trace_ref, out_ref, word_here, word_ref, column_ref, scale_ref, arrived
):
    word_here[...] = (sent_ref[...] + 0.5).astype(jnp.int32)
    words = pltpu.make_async_copy(word_here, word_ref, arrived)
    words.start()
    column_ref[...] = sent_ref[...].T
    for number in range(out_ref.shape[0]):
        column = column_ref[2 * capacity : 4 * capacity, number : number + 1]
        scale_ref[number] = jnp.broadcast_to(column, (2 * capacity, LANES))
    left = LANES - 1 - lax.broadcasted_iota(jnp.int32, (rows, LANES), 1)
    words.wait()
    for number in range(out_ref.shape[0]):
        total = [jnp.zeros((rows, LANES), jnp.float32)] * 2
        for slot in range(capacity):
            base = word_ref[number, slot]
            shift = word_ref[number, slot + capacity]
            first = scale_ref[number, slot : slot + 1, :]
            second = scale_ref[number, slot + capacity : slot + capacity + 1, :]
            stays = left >= shift
            one_kind = jnp.where(
                stays, trace_ref[pl.ds(base + 1, rows), :], trace_ref[pl.ds(base, rows), :]
            )
            base = base + 2 * rows
            other_kind = jnp.where(
                stays, trace_ref[pl.ds(base + 1, rows), :], trace_ref[pl.ds(base, rows), :]
            )
            moved = pltpu.roll(one_kind * first + other_kind * second, shift, 1)
            total[slot % 2] = total[slot % 2] + moved
        out_ref[number] = total[0] + total[1]


def smooth_kernel(rates_ref, part_ref, out_ref):
    signal = jnp.sum(part_ref[...], axis=0)
    taps = rates_ref.shape[0]
    rows = signal.shape[0]
    row = lax.broadcasted_iota(jnp.int32, (rows, LANES), 0)
    lane = lax.broadcasted_iota(jnp.int32, (rows, LANES), 1)
    previous = jnp.where(row == 0, 0.0, pltpu.roll(signal, 1, 0))
    total = [jnp.zeros_like(signal)] * 4
    for tap in range(taps):
        moved = signal
        if tap > 0:
            moved = pltpu.roll(jnp.where(lane < LANES - tap, signal, previous), tap, 1)
        total[tap % 4] = total[tap % 4] + moved * rates_ref[tap : tap + 1, :]
    out_ref[...] = (total[0] + total[1]) + (total[2] + total[3])


def local(
    green_tensor,
    mechanism,
    point_owner,
    point_row,
    onset_step,
    slip_amount,
    point_count,
    rake_angle,
    slip_rate,
):
    owners = lax.axis_size("owner")
    variations, length = point_row.shape
    points, parts, steps = green_tensor.shape
    taps = slip_rate.shape[1]
    rows = steps // LANES
    capacity = 2 * length // owners
    assert variations == 1 and capacity * FIELDS <= LANES
    listed = [point_owner.reshape(1, length), point_row, onset_step, slip_amount]
    table = pl.pallas_call(
        functools.partial(route_kernel, capacity, rows),
        out_shape=jax.ShapeDtypeStruct((owners, LANES), jnp.float32),
        in_specs=[SMEM] * 2 + [ANY] * 4,
        out_specs=VMEM,
        scratch_shapes=[pltpu.VMEM((1, length), array.dtype) for array in listed]
        + [pltpu.SemaphoreType.DMA((4,))],
        compiler_params=SMALL,
        name="route",
    )(point_count, rake_angle, *[in_hbm(array) for array in listed])
    table = lax.all_to_all(
        table.reshape(owners, 1, LANES), "owner", split_axis=0, concat_axis=0, tiled=True
    )
    group, chunk = 16, 32
    traces, rates = pl.pallas_call(
        functools.partial(project_kernel, rows, group, chunk),
        out_shape=(
            pltpu.VMEM((points * (4 * rows + 1), LANES), jnp.float32),
            pltpu.VMEM((taps, LANES), jnp.float32),
        ),
        in_specs=[ANY] * 3,
        out_specs=(VMEM, VMEM),
        scratch_shapes=[
            pltpu.VMEM((parts, 2, points), jnp.float32),
            pltpu.VMEM((1, taps), jnp.float32),
            pltpu.VMEM((parts, points, steps), jnp.bfloat16),
            pltpu.VMEM((LANES, points), jnp.float32),
            pltpu.VMEM((points, LANES), jnp.float32),
            pltpu.SemaphoreType.DMA((2,)),
            pltpu.SemaphoreType.DMA((points // chunk,)),
        ],
        compiler_params=SMALL,
        name="project",
    )(
        in_hbm(jnp.transpose(mechanism, (1, 0, 2))),
        in_hbm(slip_rate),
        in_hbm(jnp.transpose(green_tensor, (1, 0, 2))),
    )
    partial = pl.pallas_call(
        functools.partial(gather_kernel, capacity, rows),
        out_shape=pltpu.VMEM((owners, rows, LANES), jnp.float32),
        in_specs=[VMEM, VMEM],
        out_specs=VMEM,
        scratch_shapes=[
            pltpu.VMEM((owners, LANES), jnp.int32),
            pltpu.SMEM((owners, LANES), jnp.int32),
            pltpu.VMEM((LANES, owners), jnp.float32),
            pltpu.VMEM((owners, 2 * capacity, LANES), jnp.float32),
            pltpu.SemaphoreType.DMA,
        ],
        compiler_params=SMALL,
        name="gather",
    )(in_vmem(table.reshape(owners, LANES)), in_vmem(traces))
    partial = lax.all_to_all(partial, "owner", split_axis=0, concat_axis=0, tiled=True)
    result = pl.pallas_call(
        smooth_kernel,
        out_shape=jax.ShapeDtypeStruct((rows, LANES), jnp.float32),
        in_specs=[VMEM, VMEM],
        out_specs=VMEM,
        compiler_params=SMALL,
        name="smooth",
    )(in_vmem(rates), in_vmem(partial))
    return result.reshape(1, steps)


def solution(mesh):
    in_specs = (
        P(("site", "owner"), None, None),
        P(None, None, "owner"),
        P("owner", None, None),
        P("owner", None),
        P("owner", None),
        P("owner", None),
        P("owner"),
        P("owner"),
        P("owner", None),
    )
    out_specs = P(("site", "owner"), None)
    return jax.shard_map(local, mesh=mesh, in_specs=in_specs, out_specs=out_specs, check_vma=False)
```

```python
import functools

import jax
import jax.numpy as jnp
from jax import lax
from jax.experimental import pallas as pl
from jax.experimental.pallas import tpu as pltpu
from jax.sharding import PartitionSpec as P

LANES = 128
FIELDS = 4
ANY = pl.BlockSpec(memory_space=pltpu.HBM)
SMEM = pl.BlockSpec(memory_space=pltpu.SMEM)
VMEM = pl.BlockSpec(memory_space=pltpu.VMEM)
SMALL = pltpu.CompilerParams(vmem_limit_bytes=16 << 20)


def in_hbm(array):
    return pltpu.with_memory_space_constraint(array, pltpu.HBM)


def in_vmem(array):
    return pltpu.with_memory_space_constraint(array, pltpu.VMEM)


def fetch(sources, targets, arrived):
    copies = [
        pltpu.make_async_copy(source, target, arrived.at[number])
        for number, (source, target) in enumerate(zip(sources, targets))
    ]
    for copy in copies:
        copy.start()
    for copy in copies:
        copy.wait()


def route_kernel(capacity, rows, *refs):
    count_ref, rake_ref, sources, out_ref, targets, arrived = (
        refs[0], refs[1], refs[2:6], refs[6], refs[7:11], refs[11]
    )
    fetch(sources, targets, arrived)
    owner_ref, row_ref, onset_ref, slip_ref = targets
    owners = out_ref.shape[0]
    length = row_ref.shape[1]
    lane = lax.broadcasted_iota(jnp.int32, (1, length), 1)
    alive = lane < count_ref[0]
    owner_index = lax.broadcasted_iota(jnp.int32, (owners, length), 0)
    hot = ((owner_index == owner_ref[...]) & alive).astype(jnp.float32)
    earlier = lax.broadcasted_iota(jnp.int32, (length, length), 0) < lax.broadcasted_iota(
        jnp.int32, (length, length), 1
    )
    before = jnp.dot(
        hot.astype(jnp.bfloat16), earlier.astype(jnp.bfloat16), preferred_element_type=jnp.float32
    )
    rank = jnp.sum(hot * before, axis=0, keepdims=True).astype(jnp.int32)
    onset = onset_ref[...]
    whole = onset >> (LANES.bit_length() - 1)
    base = row_ref[...] * (4 * rows + 1) + (rows - 1) - whole
    rake = jnp.full((1, length), rake_ref[0], jnp.float32)
    weight = jnp.where(alive, slip_ref[...], 0.0)
    fields = (
        base.astype(jnp.float32),
        (onset & (LANES - 1)).astype(jnp.float32),
        jnp.cos(rake) * weight,
        jnp.sin(rake) * weight,
    )
    place = lax.broadcasted_iota(jnp.int32, (len(fields) * capacity, length), 0)
    pieces = []
    for field in fields:
        piece = []
        for _ in range(3):
            piece.append(field.astype(jnp.bfloat16).astype(jnp.float32))
            field = field - piece[-1]
        pieces.append(piece)
    total = None
    for part in range(3):
        spread = jnp.zeros(place.shape, jnp.float32)
        for number, piece in enumerate(pieces):
            spread = jnp.where(place == rank + number * capacity, piece[part], spread)
        term = lax.dot_general(
            hot.astype(jnp.bfloat16),
            spread.astype(jnp.bfloat16),
            (((1,), (1,)), ((), ())),
            preferred_element_type=jnp.float32,
        )
        total = term if part == 0 else total + term
    out_ref[...] = jnp.zeros_like(out_ref)
    out_ref[:, 0 : total.shape[1]] = total


def project_kernel(
    rows, group, chunk, mech_ref, rate_ref, green_ref, out_ref, rates_ref,
    mech_here, rate_here, green_here, flat_ref, column_ref, arrived, landed,
):
    parts, points, _ = green_ref.shape
    small = [
        pltpu.make_async_copy(mech_ref, mech_here, arrived.at[0]),
        pltpu.make_async_copy(rate_ref, rate_here, arrived.at[1]),
    ]
    large = [
        pltpu.make_async_copy(
            green_ref.at[:, pl.ds(first, chunk), :], green_here.at[:, pl.ds(first, chunk), :], landed.at[number]
        )
        for number, first in enumerate(range(0, points, chunk))
    ]
    for copy in small + large:
        copy.start()
    pitch = 4 * rows + 1
    blank = jnp.zeros((rows, LANES), jnp.float32)

    def clear(number, carry):
        for kind in range(2):
            out_ref[pl.ds(number * pitch + kind * 2 * rows, rows), :] = blank
        return carry

    lax.fori_loop(0, points, clear, 0, unroll=8)
    flat_ref[...] = jnp.zeros_like(flat_ref)
    for copy in small:
        copy.wait()
    taps = rate_here.shape[1]
    for part in range(parts):
        for kind in range(2):
            flat_ref[2 * part + kind : 2 * part + kind + 1, :] = mech_here[part, kind : kind + 1, :]
    flat_ref[2 * parts : 2 * parts + 1, 0:taps] = rate_here[...]
    column_ref[...] = flat_ref[...].T
    rates_ref[...] = jnp.broadcast_to(column_ref[0:taps, 2 * parts : 2 * parts + 1], (taps, LANES))

    def one(number, carry):
        first = pl.multiple_of(number * group, group)
        for half in range(0, group, 8):
            corner = (first + half) * pitch + rows
            scale = [
                jnp.broadcast_to(column_ref[pl.ds(first + half, 8), i : i + 1], (8, LANES))
                for i in range(2 * parts)
            ]
            for step in range(rows):
                total = [None, None]
                for part in range(parts):
                    block = green_here[part, pl.ds(first, group), step * LANES : (step + 1) * LANES]
                    block = block.astype(jnp.float32)[half : half + 8]
                    for kind in range(2):
                        term = scale[2 * part + kind] * block
                        total[kind] = term if part == 0 else total[kind] + term
                for kind in range(2):
                    kept = total[kind].astype(jnp.bfloat16).astype(jnp.float32)
                    out_ref[pl.ds(corner + 2 * kind * rows + step, 8, stride=pitch), :] = kept
        return carry

    for number, copy in enumerate(large):
        copy.wait()
        lax.fori_loop(number * (chunk // group), (number + 1) * (chunk // group), one, 0)


def gather_kernel(
    capacity, rows, sent_ref, trace_ref, out_ref, word_here, word_ref, column_ref, scale_ref, arrived
):
    word_here[...] = (sent_ref[...] + 0.5).astype(jnp.int32)
    words = pltpu.make_async_copy(word_here, word_ref, arrived)
    words.start()
    column_ref[...] = sent_ref[...].T
    for number in range(out_ref.shape[0]):
        column = column_ref[2 * capacity : 4 * capacity, number : number + 1]
        scale_ref[number] = jnp.broadcast_to(column, (2 * capacity, LANES))
    left = LANES - 1 - lax.broadcasted_iota(jnp.int32, (rows, LANES), 1)
    words.wait()
    for number in range(out_ref.shape[0]):
        total = [jnp.zeros((rows, LANES), jnp.float32)] * 2
        for slot in range(capacity):
            base = word_ref[number, slot]
            shift = word_ref[number, slot + capacity]
            first = scale_ref[number, slot : slot + 1, :]
            second = scale_ref[number, slot + capacity : slot + capacity + 1, :]
            stays = left >= shift
            one_kind = jnp.where(
                stays, trace_ref[pl.ds(base + 1, rows), :], trace_ref[pl.ds(base, rows), :]
            )
            base = base + 2 * rows
            other_kind = jnp.where(
                stays, trace_ref[pl.ds(base + 1, rows), :], trace_ref[pl.ds(base, rows), :]
            )
            moved = pltpu.roll(one_kind * first + other_kind * second, shift, 1)
            total[slot % 2] = total[slot % 2] + moved
        out_ref[number] = total[0] + total[1]


def smooth_kernel(rates_ref, part_ref, out_ref):
    signal = jnp.sum(part_ref[...], axis=0)
    taps = rates_ref.shape[0]
    rows = signal.shape[0]
    row = lax.broadcasted_iota(jnp.int32, (rows, LANES), 0)
    lane = lax.broadcasted_iota(jnp.int32, (rows, LANES), 1)
    previous = jnp.where(row == 0, 0.0, pltpu.roll(signal, 1, 0))
    total = [jnp.zeros_like(signal)] * 4
    for tap in range(taps):
        moved = signal
        if tap > 0:
            moved = pltpu.roll(jnp.where(lane < LANES - tap, signal, previous), tap, 1)
        total[tap % 4] = total[tap % 4] + moved * rates_ref[tap : tap + 1, :]
    out_ref[...] = (total[0] + total[1]) + (total[2] + total[3])


def local(
    green_tensor,
    mechanism,
    point_owner,
    point_row,
    onset_step,
    slip_amount,
    point_count,
    rake_angle,
    slip_rate,
):
    owners = lax.axis_size("owner")
    variations, length = point_row.shape
    points, parts, steps = green_tensor.shape
    taps = slip_rate.shape[1]
    rows = steps // LANES
    capacity = 2 * length // owners
    assert variations == 1 and capacity * FIELDS <= LANES
    listed = [point_owner.reshape(1, length), point_row, onset_step, slip_amount]
    table = pl.pallas_call(
        functools.partial(route_kernel, capacity, rows),
        out_shape=jax.ShapeDtypeStruct((owners, LANES), jnp.float32),
        in_specs=[SMEM] * 2 + [ANY] * 4,
        out_specs=VMEM,
        scratch_shapes=[pltpu.VMEM((1, length), array.dtype) for array in listed]
        + [pltpu.SemaphoreType.DMA((4,))],
        compiler_params=SMALL,
        name="route",
    )(point_count, rake_angle, *[in_hbm(array) for array in listed])
    table = lax.all_to_all(
        table.reshape(owners, 1, LANES), "owner", split_axis=0, concat_axis=0, tiled=True
    )
    group, chunk = 16, 32
    traces, rates = pl.pallas_call(
        functools.partial(project_kernel, rows, group, chunk),
        out_shape=(
            pltpu.VMEM((points * (4 * rows + 1), LANES), jnp.float32),
            pltpu.VMEM((taps, LANES), jnp.float32),
        ),
        in_specs=[ANY] * 3,
        out_specs=(VMEM, VMEM),
        scratch_shapes=[
            pltpu.VMEM((parts, 2, points), jnp.float32),
            pltpu.VMEM((1, taps), jnp.float32),
            pltpu.VMEM((parts, points, steps), jnp.bfloat16),
            pltpu.VMEM((LANES, points), jnp.float32),
            pltpu.VMEM((points, LANES), jnp.float32),
            pltpu.SemaphoreType.DMA((2,)),
            pltpu.SemaphoreType.DMA((points // chunk,)),
        ],
        compiler_params=SMALL,
        name="project",
    )(
        in_hbm(jnp.transpose(mechanism, (1, 0, 2))),
        in_hbm(slip_rate),
        in_hbm(jnp.transpose(green_tensor, (1, 0, 2))),
    )
    partial = pl.pallas_call(
        functools.partial(gather_kernel, capacity, rows),
        out_shape=pltpu.VMEM((owners, rows, LANES), jnp.float32),
        in_specs=[VMEM, VMEM],
        out_specs=VMEM,
        scratch_shapes=[
            pltpu.VMEM((owners, LANES), jnp.int32),
            pltpu.SMEM((owners, LANES), jnp.int32),
            pltpu.VMEM((LANES, owners), jnp.float32),
            pltpu.VMEM((owners, 2 * capacity, LANES), jnp.float32),
            pltpu.SemaphoreType.DMA,
        ],
        compiler_params=pltpu.CompilerParams(vmem_limit_bytes=16 << 20),
        name="gather",
    )(in_vmem(table.reshape(owners, LANES)), in_vmem(traces))
    partial = lax.all_to_all(partial, "owner", split_axis=0, concat_axis=0, tiled=True)
    result = pl.pallas_call(
        smooth_kernel,
        out_shape=jax.ShapeDtypeStruct((rows, LANES), jnp.float32),
        in_specs=[VMEM, VMEM],
        out_specs=VMEM,
        compiler_params=SMALL,
        name="smooth",
    )(in_vmem(rates), in_vmem(partial))
    return result.reshape(1, steps)


def solution(mesh):
    in_specs = (
        P(("site", "owner"), None, None),
        P(None, None, "owner"),
        P("owner", None, None),
        P("owner", None),
        P("owner", None),
        P("owner", None),
        P("owner"),
        P("owner"),
        P("owner", None),
    )
    out_specs = P(("site", "owner"), None)
    return jax.shard_map(local, mesh=mesh, in_specs=in_specs, out_specs=out_specs, check_vma=False)
```
